32 devices in a mesh: shot: 4 (over y, core), gx: 4 (over z), gy: 2 (over x).
Axes of the slice: x: 2, y: 2, z: 4, core: 2. Of those that a mesh axis runs over, the one named last changes fastest.
Arguments:
- latent: float32 [32, 24, 1024], P('shot', 'gx', 'gy'), may hold values from -6 to 6
- w_first: float32 [64, 64], replicated, may hold values from -0.75 to 0.75
- w_second: float32 [64, 128], replicated, may hold values from -0.75 to 0.75
- fwd_press: float32 [4, 96, 64, 128], P('shot', 'gx', 'gy'), may hold values from -1.5 to 8
- fwd_vel: float32 [4, 3, 96, 64, 128], P('shot', None, 'gx', 'gy'), may hold values from -1.5 to 8
- adj_press: float32 [4, 96, 64, 128], P('shot', 'gx', 'gy'), may hold values from -1.5 to 8
- adj_vel: float32 [4, 3, 96, 64, 128], P('shot', None, 'gx', 'gy'), may hold values from -1.5 to 8
- src_pos: int32 [3, 4], P(None, 'shot'), may hold values from 0 to 127, as said below
- src_amp: float32 [3, 4], P(None, 'shot'), may hold values from -24 to 24
- rec_pos: int32 [4, 3, 2048], P('shot'), may hold values from 0 to 127, as said below
- observed: float32 [4, 3, 2048], P('shot'), may hold values from -6 to 6
Outputs:
- grad_latent: float32 [32, 24, 1024], P('shot', 'gx', 'gy')
- grad_first: float32 [64, 64], replicated
- grad_second: float32 [64, 128], replicated
The draws below stay inside these ranges and needn't reach their ends.
Inputs may be any that keep to these rules, and one draw needn't show every extreme that they name: `src_pos`: row 0 is an x cell below 96, row 1 a y cell below 64, row 2 a depth cell below 128. `rec_pos`: component 0 is an x cell below 96, component 1 a y cell below 64, component 2 a depth cell below 128; cells may repeat.
All inputs are finite; a program needn't handle non-finite values.
Results may differ from the reference program's by a relative error of at most 0.0003.
Values sent between devices are 32-bit elements; how exact they have to be, the bound alone decides.
A program may use at most 64 MiB of HBM per device.

```python
import jax
import jax.numpy as jnp
from jax import lax

NZ = 128
NREC = 2048
CH = 64
STEPS = 3
OUTS = 128
NX = 96
NY = 64
SHOTS = 4
XC = 24
YC = 16
ZC = 32


def draw_src_pos(key, part):
    subkeys = jax.random.split(jax.random.fold_in(key, 11), 3)
    along_x = jax.random.randint(subkeys[0], (SHOTS,), 0, NX).at[0].set(NX - 1).at[1].set(0)
    along_y = jax.random.randint(subkeys[1], (SHOTS,), 0, NY).at[0].set(NY - 1)
    along_z = jax.random.randint(subkeys[2], (SHOTS,), 0, NZ).at[0].set(NZ - 1)
    return jnp.stack([along_x, along_y, along_z]).astype(jnp.int32)


def draw_rec_pos(key, part):
    subkeys = jax.random.split(jax.random.fold_in(key, 23), 3)
    along_x = jax.random.randint(subkeys[0], (SHOTS, NREC), 0, NX).at[:, 0].set(NX - 1).at[:, 1].set(0)
    along_y = jax.random.randint(subkeys[1], (SHOTS, NREC), 0, NY).at[:, 0].set(NY - 1)
    along_z = jax.random.randint(subkeys[2], (SHOTS, NREC), 0, NZ).at[:, 0].set(NZ - 1)
    return jnp.stack([along_x, along_y, along_z], axis=1).astype(jnp.int32)


def smooth_along(values_in, axis_id, spread):
    length = values_in.shape[axis_id]
    places = jnp.arange(length, dtype=jnp.float32)
    kernel = jnp.exp(-0.5 * jnp.square((places[:, None] - places[None, :]) / spread))
    kernel = kernel / jnp.sum(kernel, axis=1, keepdims=True)
    rotated = jnp.moveaxis(values_in, axis_id, -1)
    return jnp.moveaxis(jnp.dot(rotated, kernel.T), -1, axis_id)


def taper(length):
    places = jnp.arange(length, dtype=jnp.float32)
    distance = jnp.minimum(places, length - 1.0 - places)
    return jnp.square(jnp.sin(0.5 * jnp.pi * jnp.minimum(1.0, (distance + 0.5) / 6.0)))


def wavefield(key, leading):
    subkeys = jax.random.split(key, 2)
    full_shape = leading + (NX, NY, NZ)
    dimensions = len(full_shape)
    white_noise = jax.random.normal(subkeys[0], full_shape, jnp.float32)
    spread = 3.0
    smooth = white_noise
    for axis_id in (dimensions - 3, dimensions - 2, dimensions - 1):
        smooth = smooth_along(smooth, axis_id, spread)
    smooth = smooth / jnp.sqrt(jnp.mean(jnp.square(smooth)) + 1e-12)
    smooth = jnp.clip(smooth, -3.0, 3.0)
    envelope = taper(NX)[:, None, None] * taper(NY)[None, :, None] * taper(NZ)[None, None, :]
    rough_part = 0.12 * jax.random.normal(subkeys[1], full_shape, jnp.float32)
    wave_field = envelope * (2.5 + smooth) + rough_part
    return jnp.clip(wave_field, -1.5, 8.0).astype(jnp.float32)


def draw_fwd_press(key, part):
    return wavefield(jax.random.fold_in(key, 31), (SHOTS,))


def draw_fwd_vel(key, part):
    return wavefield(jax.random.fold_in(key, 37), (SHOTS, 3))


def draw_adj_press(key, part):
    return wavefield(jax.random.fold_in(key, 41), (SHOTS,))


def draw_adj_vel(key, part):
    return wavefield(jax.random.fold_in(key, 43), (SHOTS, 3))


def shard_levels(key, dims, cuts, smallest, high):
    def one(position, blocks):
        steps = jax.random.uniform(jax.random.fold_in(jax.random.fold_in(key, 6), position), (blocks,), jnp.float32, smallest / len(cuts), high / len(cuts))
        return jnp.repeat(jnp.exp(steps), dims[position] // blocks).reshape((-1,) + (1,) * (len(dims) - position - 1))

    loudness = one(*cuts[0])
    for cut in cuts[1:]:
        loudness = loudness * one(*cut)
    return loudness


def scatter_about(key, extent, width, reach, cuts=(), kind=jnp.bfloat16):
    level = shard_levels(key, extent, cuts, -0.22, 0.18) if cuts else 1.0
    result = jax.random.normal(key, extent, jnp.float32) * width * level
    return jnp.minimum(jnp.maximum(result, -reach), reach).astype(kind)


def setup_inputs(seed: int = 0) -> dict:
    streams_of = jax.random.split(jax.random.key(seed), 12)
    latent = scatter_about(streams_of[0], (ZC, XC, YC * CH), 1.0, 6.0, ((0, 4), (1, 4), (2, 2)), jnp.float32)
    w_first = scatter_about(streams_of[1], (CH, CH), CH ** -0.5, 0.75, (), jnp.float32)
    w_second = scatter_about(streams_of[2], (CH, OUTS), CH ** -0.5, 0.75, (), jnp.float32)
    fwd_press = draw_fwd_press(jax.random.fold_in(streams_of[11], 71), 0)
    fwd_vel = draw_fwd_vel(jax.random.fold_in(streams_of[11], 71), 0)
    adj_press = draw_adj_press(jax.random.fold_in(streams_of[11], 71), 0)
    adj_vel = draw_adj_vel(jax.random.fold_in(streams_of[11], 71), 0)
    src_pos = draw_src_pos(jax.random.fold_in(streams_of[11], 71), 0)
    src_amp = scatter_about(streams_of[8], (STEPS, SHOTS), 4.0, 24.0, ((1, 4),), jnp.float32)
    rec_pos = draw_rec_pos(jax.random.fold_in(streams_of[11], 71), 0)
    observed = scatter_about(streams_of[10], (SHOTS, STEPS, NREC), 1.0, 6.0, ((0, 4),), jnp.float32)
    return dict(latent=latent, w_first=w_first, w_second=w_second, fwd_press=fwd_press, fwd_vel=fwd_vel, adj_press=adj_press, adj_vel=adj_vel, src_pos=src_pos, src_amp=src_amp, rec_pos=rec_pos, observed=observed)


coeffs = (1225.0 / 1024.0, -245.0 / 3072.0, 49.0 / 5120.0, -5.0 / 7168.0)


def take_slab(values_in, axis_id, start_at, length):
    return lax.slice_in_dim(values_in, start_at, start_at + length, axis=axis_id)


def diff_plus(extended, axis_id, start_at, length):
    summed = 0.0
    for order, weight in enumerate(coeffs):
        offset = order + 1
        summed = summed + weight * (take_slab(extended, axis_id, start_at + offset, length) - take_slab(extended, axis_id, start_at - offset + 1, length))
    return summed


def diff_minus(extended, axis_id, start_at, length):
    summed = 0.0
    for order, weight in enumerate(coeffs):
        offset = order + 1
        summed = summed + weight * (take_slab(extended, axis_id, start_at + offset - 1, length) - take_slab(extended, axis_id, start_at - offset, length))
    return summed


def edge_pad(field_in, axis_id):
    widths = [(0, 0), (0, 0), (0, 0)]
    widths[axis_id] = (4, 4)
    return jnp.pad(field_in, widths)


def wave_step(pressure, vel_x, vel_y, vel_z, modulus, buoyancy):
    size_x, size_y, size_z = pressure.shape
    grad_x = diff_plus(edge_pad(pressure, 0), 0, 4, size_x)
    grad_y = diff_plus(edge_pad(pressure, 1), 1, 4, size_y)
    grad_z = diff_plus(edge_pad(pressure, 2), 2, 4, size_z)
    vel_x = vel_x - buoyancy * grad_x
    vel_y = vel_y - buoyancy * grad_y
    vel_z = vel_z - buoyancy * grad_z
    diverge = diff_minus(edge_pad(vel_x, 0), 0, 4, size_x) + diff_minus(edge_pad(vel_y, 1), 1, 4, size_y) + diff_minus(edge_pad(vel_z, 2), 2, 4, size_z)
    pressure = pressure - modulus * diverge
    return pressure, vel_x, vel_y, vel_z, diverge, grad_x, grad_y, grad_z


def decode(latent, w_first, w_second):
    depth_c, rows_x, merged = latent.shape
    rows_y = merged // CH
    flattened = latent.reshape(-1, CH)
    hidden = jnp.tanh(jnp.dot(flattened, w_first, precision=lax.Precision.HIGHEST))
    outputs = jnp.dot(hidden, w_second, precision=lax.Precision.HIGHEST)
    fine_out = outputs.reshape(depth_c, rows_x, rows_y, 2, 4, 4, 4).transpose(3, 1, 4, 2, 5, 0, 6).reshape(2, rows_x * 4, rows_y * 4, depth_c * 4)
    return flattened, hidden, fine_out


def materials(fine_out):
    wave_speed = 0.15 + 0.25 * jax.nn.sigmoid(fine_out[0])
    density = 1.0 + 1.5 * jax.nn.sigmoid(fine_out[1])
    return density * wave_speed * wave_speed, 1.0 / density


def decoder_grads(flattened, hidden, fine_out, grad_mod, grad_buoy, w_first, w_second):
    sig_speed = jax.nn.sigmoid(fine_out[0])
    sig_dens = jax.nn.sigmoid(fine_out[1])
    wave_speed = 0.15 + 0.25 * sig_speed
    density = 1.0 + 1.5 * sig_dens
    grad_speed = grad_mod * 2.0 * density * wave_speed
    grad_dens = grad_mod * wave_speed * wave_speed - grad_buoy / (density * density)
    grad_fine = jnp.stack([grad_speed * 0.25 * sig_speed * (1.0 - sig_speed), grad_dens * 1.5 * sig_dens * (1.0 - sig_dens)])
    size_x, size_y, size_z = grad_fine.shape[1], grad_fine.shape[2], grad_fine.shape[3]
    grad_out = grad_fine.reshape(2, size_x // 4, 4, size_y // 4, 4, size_z // 4, 4).transpose(5, 1, 3, 0, 2, 4, 6).reshape(-1, 128)
    grad_hidden = jnp.dot(grad_out, w_second.T, precision=lax.Precision.HIGHEST)
    grad_pre = grad_hidden * (1.0 - hidden * hidden)
    grad_latent = jnp.dot(grad_pre, w_first.T, precision=lax.Precision.HIGHEST).reshape(size_z // 4, size_x // 4, (size_y // 4) * CH)
    grad_second = jnp.dot(hidden.T, grad_out, precision=lax.Precision.HIGHEST)
    grad_first = jnp.dot(flattened.T, grad_pre, precision=lax.Precision.HIGHEST)
    return grad_latent, grad_first, grad_second


def reference(latent, w_first, w_second, fwd_press, fwd_vel, adj_press, adj_vel, src_pos, src_amp, rec_pos, observed):
    flattened, hidden, fine_out = decode(latent, w_first, w_second)
    modulus, buoyancy = materials(fine_out)

    def one_shot(totals, inputs):
        grad_mod, grad_buoy = totals
        start_press, start_vel, back_press, back_vel, source, amplitudes, receivers, observed_now = inputs
        pressure, vel_x, vel_y, vel_z = start_press, start_vel[0], start_vel[1], start_vel[2]
        stored = []
        misfits = []
        for moment in range(STEPS):
            pressure, vel_x, vel_y, vel_z, diverge, grad_x, grad_y, grad_z = wave_step(pressure, vel_x, vel_y, vel_z, modulus, buoyancy)
            pressure = pressure.at[source[0], source[1], source[2]].add(amplitudes[moment])
            misfits.append(pressure[receivers[0], receivers[1], receivers[2]] - observed_now[moment])
            stored.append((diverge, grad_x, grad_y, grad_z))
        pressure, vel_x, vel_y, vel_z = back_press, back_vel[0], back_vel[1], back_vel[2]
        for moment in reversed(range(STEPS)):
            pressure = pressure.at[receivers[0], receivers[1], receivers[2]].add(misfits[moment])
            pressure, vel_x, vel_y, vel_z, diverge, grad_x, grad_y, grad_z = wave_step(pressure, vel_x, vel_y, vel_z, modulus, buoyancy)
            grad_mod = grad_mod - pressure * stored[moment][0]
            grad_buoy = grad_buoy - (vel_x * stored[moment][1] + vel_y * stored[moment][2] + vel_z * stored[moment][3])
        return (grad_mod, grad_buoy), None

    zeros = jnp.zeros(modulus.shape, jnp.float32)
    totals, _ignored = lax.scan(one_shot, (zeros, zeros), (fwd_press, fwd_vel, adj_press, adj_vel, src_pos.T, src_amp.T, rec_pos, observed))
    grad_latent, grad_first, grad_second = decoder_grads(flattened, hidden, fine_out, totals[0], totals[1], w_first, w_second)
    return grad_latent, grad_first, grad_second
```

```python
import jax
import jax.numpy as jnp
from jax import lax
from jax.sharding import PartitionSpec as P

CH = 64
STEPS = 3


coeffs = (1225.0 / 1024.0, -245.0 / 3072.0, 49.0 / 5120.0, -5.0 / 7168.0)


def with_halo(block, sides, width):
    for axis, dim in sides:
        count = lax.axis_size(axis)
        forward = [(i, i + 1) for i in range(count - 1)]
        backward = [(target, source) for source, target in forward]
        low = lax.ppermute(
            lax.slice_in_dim(block, block.shape[dim] - width, None, axis=dim), axis, forward
        )
        high = lax.ppermute(lax.slice_in_dim(block, 0, width, axis=dim), axis, backward)
        block = jnp.concatenate([low, block, high], axis=dim)
    return block


def take_slab(values_in, axis_id, start_at, length):
    return lax.slice_in_dim(values_in, start_at, start_at + length, axis=axis_id)


def diff_plus(extended, axis_id, start_at, length):
    summed = 0.0
    for order, weight in enumerate(coeffs):
        offset = order + 1
        summed = summed + weight * (
            take_slab(extended, axis_id, start_at + offset, length)
            - take_slab(extended, axis_id, start_at - offset + 1, length)
        )
    return summed


def diff_minus(extended, axis_id, start_at, length):
    summed = 0.0
    for order, weight in enumerate(coeffs):
        offset = order + 1
        summed = summed + weight * (
            take_slab(extended, axis_id, start_at + offset - 1, length)
            - take_slab(extended, axis_id, start_at - offset, length)
        )
    return summed


def depth_pad(field_in):
    return jnp.pad(field_in, ((0, 0), (0, 0), (4, 4)))


def rim_x(field_in):
    return with_halo(field_in, (("gx", 0),), 4)


def rim_y(field_in):
    return with_halo(field_in, (("gy", 1),), 4)


def wide_step(fields, modulus, buoy_x, buoy_y, buoyancy):
    pressure, ext_x, ext_y, vel_z = fields
    size_x, size_y, size_z = pressure.shape
    slope_x = diff_plus(with_halo(pressure, (("gx", 0),), 8), 0, 4, size_x + 8)
    slope_y = diff_plus(with_halo(pressure, (("gy", 1),), 8), 1, 4, size_y + 8)
    grad_z = diff_plus(depth_pad(pressure), 2, 4, size_z)
    ext_x = ext_x - buoy_x * slope_x
    ext_y = ext_y - buoy_y * slope_y
    vel_z = vel_z - buoyancy * grad_z
    diverge = (
        diff_minus(ext_x, 0, 4, size_x)
        + diff_minus(ext_y, 1, 4, size_y)
        + diff_minus(depth_pad(vel_z), 2, 4, size_z)
    )
    pressure = pressure - modulus * diverge
    slopes = (slope_x[4 : 4 + size_x], slope_y[:, 4 : 4 + size_y], grad_z)
    own_vel = (ext_x[4 : 4 + size_x], ext_y[:, 4 : 4 + size_y], vel_z)
    return ((pressure, ext_x, ext_y, vel_z), diverge, slopes, own_vel)


def decode(latent, w_first, w_second):
    depth_c, rows_x, merged = latent.shape
    rows_y = merged // CH
    flattened = latent.reshape(-1, CH)
    hidden = jnp.tanh(jnp.dot(flattened, w_first, precision=lax.Precision.HIGHEST))
    outputs = jnp.dot(hidden, w_second, precision=lax.Precision.HIGHEST)
    fine_out = (
        outputs.reshape(depth_c, rows_x, rows_y, 2, 4, 4, 4)
        .transpose(3, 1, 4, 2, 5, 0, 6)
        .reshape(2, rows_x * 4, rows_y * 4, depth_c * 4)
    )
    return (flattened, hidden, fine_out)


def materials(fine_out):
    wave_speed = 0.15 + 0.25 * jax.nn.sigmoid(fine_out[0])
    density = 1.0 + 1.5 * jax.nn.sigmoid(fine_out[1])
    return (density * wave_speed * wave_speed, 1.0 / density)


def decoder_grads(flattened, hidden, fine_out, grad_mod, grad_buoy, w_first, w_second):
    sig_speed = jax.nn.sigmoid(fine_out[0])
    sig_dens = jax.nn.sigmoid(fine_out[1])
    wave_speed = 0.15 + 0.25 * sig_speed
    density = 1.0 + 1.5 * sig_dens
    grad_speed = grad_mod * 2.0 * density * wave_speed
    grad_dens = grad_mod * wave_speed * wave_speed - grad_buoy / (density * density)
    grad_fine = jnp.stack(
        [
            grad_speed * 0.25 * sig_speed * (1.0 - sig_speed),
            grad_dens * 1.5 * sig_dens * (1.0 - sig_dens),
        ]
    )
    size_x, size_y, size_z = (grad_fine.shape[1], grad_fine.shape[2], grad_fine.shape[3])
    grad_out = (
        grad_fine.reshape(2, size_x // 4, 4, size_y // 4, 4, size_z // 4, 4)
        .transpose(5, 1, 3, 0, 2, 4, 6)
        .reshape(-1, 128)
    )
    grad_hidden = jnp.dot(grad_out, w_second.T, precision=lax.Precision.HIGHEST)
    grad_pre = grad_hidden * (1.0 - hidden * hidden)
    grad_latent = jnp.dot(grad_pre, w_first.T, precision=lax.Precision.HIGHEST).reshape(
        size_z // 4, size_x // 4, size_y // 4 * CH
    )
    grad_second = jnp.dot(hidden.T, grad_out, precision=lax.Precision.HIGHEST)
    grad_first = jnp.dot(flattened.T, grad_pre, precision=lax.Precision.HIGHEST)
    return (grad_latent, grad_first, grad_second)


def receiver_fields(receivers, observed_now, anchor_x, anchor_y, size_x, size_y, size_z):
    local_x = receivers[0] - anchor_x
    local_y = receivers[1] - anchor_y
    inside = (local_x >= 0) & (local_x < size_x) & (local_y >= 0) & (local_y < size_y)
    column = jnp.where(inside, local_x * size_y + local_y, -1)
    count = column.shape[0]
    picks = (
        lax.broadcasted_iota(jnp.int32, (size_x * size_y, count), 0) == column[None, :]
    ).astype(jnp.bfloat16)
    depth = (
        lax.broadcasted_iota(jnp.int32, (count, size_z), 1) == receivers[2][:, None]
    ).astype(jnp.float32)
    high = lax.reduce_precision(observed_now, 8, 7)
    low = lax.reduce_precision(observed_now - high, 8, 7)
    parts = [depth]
    for moment in range(STEPS):
        parts = parts + [depth * high[moment][:, None], depth * low[moment][:, None]]
    weights = jnp.concatenate(parts, axis=1).astype(jnp.bfloat16)
    summed = jnp.dot(picks, weights, preferred_element_type=jnp.float32)
    planes = summed.reshape(size_x, size_y, len(parts), size_z)
    recorded = [planes[:, :, 1 + 2 * m] + planes[:, :, 2 + 2 * m] for m in range(STEPS)]
    return planes[:, :, 0], recorded


def body(
    latent,
    w_first,
    w_second,
    fwd_press,
    fwd_vel,
    adj_press,
    adj_vel,
    src_pos,
    src_amp,
    rec_pos,
    observed,
):
    size_x, size_y = (fwd_press.shape[1], fwd_press.shape[2])
    anchor_x = lax.axis_index("gx") * size_x
    anchor_y = lax.axis_index("gy") * size_y
    flattened, hidden, fine_out = decode(latent, w_first, w_second)
    slab_mod, slab_buoy = materials(fine_out)
    stacked = lax.all_gather(jnp.stack([slab_mod, slab_buoy]), "shot", axis=3, tiled=True)
    modulus, buoyancy = (stacked[0], stacked[1])
    buoy_x = rim_x(buoyancy)
    buoy_y = rim_y(buoyancy)

    def prepare(vel_x, vel_y):
        return (rim_x(vel_x), rim_y(vel_y))

    def advance(fields):
        return wide_step(fields, modulus, buoy_x, buoy_y, buoyancy)

    def one_shot(totals, inputs):
        grad_mod, grad_buoy = totals
        (
            start_press,
            start_vel,
            back_press,
            back_vel,
            source,
            amplitudes,
            receivers,
            observed_now,
        ) = inputs
        size_z = start_press.shape[2]
        at_source = (
            (lax.broadcasted_iota(jnp.int32, start_press.shape, 0) == source[0] - anchor_x)
            & (lax.broadcasted_iota(jnp.int32, start_press.shape, 1) == source[1] - anchor_y)
            & (lax.broadcasted_iota(jnp.int32, start_press.shape, 2) == source[2])
        )
        hits, recorded = receiver_fields(
            receivers, observed_now, anchor_x, anchor_y, size_x, size_y, size_z
        )
        fields = (start_press,) + prepare(start_vel[0], start_vel[1]) + (start_vel[2],)
        stored = []
        misfits = []
        for moment in range(STEPS):
            fields, diverge, slopes, own_vel = advance(fields)
            pressure = fields[0] + jnp.where(at_source, amplitudes[moment], 0.0)
            fields = (pressure,) + fields[1:]
            misfits.append(hits * pressure - recorded[moment])
            stored.append((diverge, slopes))
        fields = (back_press,) + prepare(back_vel[0], back_vel[1]) + (back_vel[2],)
        for moment in reversed(range(STEPS)):
            pressure = fields[0] + misfits[moment]
            fields, diverge, slopes, own_vel = advance((pressure,) + fields[1:])
            grad_mod = grad_mod - fields[0] * stored[moment][0]
            grad_buoy = grad_buoy - (
                own_vel[0] * stored[moment][1][0]
                + own_vel[1] * stored[moment][1][1]
                + own_vel[2] * stored[moment][1][2]
            )
        return ((grad_mod, grad_buoy), None)

    zeros = jnp.zeros(modulus.shape, jnp.float32)
    totals, _ignored = lax.scan(
        one_shot,
        (zeros, zeros),
        (fwd_press, fwd_vel, adj_press, adj_vel, src_pos.T, src_amp.T, rec_pos, observed),
    )
    shares = lax.psum_scatter(
        jnp.stack([totals[0], totals[1]]), "shot", scatter_dimension=3, tiled=True
    )
    grad_latent, grad_first, grad_second = decoder_grads(
        flattened, hidden, fine_out, shares[0], shares[1], w_first, w_second
    )
    grad_first, grad_second = lax.psum((grad_first, grad_second), ("shot", "gx", "gy"))
    return (grad_latent, grad_first, grad_second)


def solution(mesh):
    in_specs = (
        P("shot", "gx", "gy"),
        P(),
        P(),
        P("shot", "gx", "gy", None),
        P("shot", None, "gx", "gy", None),
        P("shot", "gx", "gy", None),
        P("shot", None, "gx", "gy", None),
        P(None, "shot"),
        P(None, "shot"),
        P("shot", None, None),
        P("shot", None, None),
    )
    out_specs = (P("shot", "gx", "gy"), P(), P())
    return jax.shard_map(body, mesh=mesh, in_specs=in_specs, out_specs=out_specs, check_vma=False)
```

```python
import jax
import jax.numpy as jnp
from jax import lax
from jax.experimental import pallas as pl
from jax.experimental.pallas import tpu as pltpu
from jax.sharding import PartitionSpec as P

CH = 64
STEPS = 3


coeffs = (1225.0 / 1024.0, -245.0 / 3072.0, 49.0 / 5120.0, -5.0 / 7168.0)


def decode(latent, w_first, w_second):
    depth_c, rows_x, merged = latent.shape
    rows_y = merged // CH
    flattened = latent.reshape(-1, CH)
    hidden = jnp.tanh(jnp.dot(flattened, w_first, precision=lax.Precision.HIGHEST))
    outputs = jnp.dot(hidden, w_second, precision=lax.Precision.HIGHEST)
    fine_out = (
        outputs.reshape(depth_c, rows_x, rows_y, 2, 4, 4, 4)
        .transpose(3, 1, 4, 2, 5, 0, 6)
        .reshape(2, rows_x * 4, rows_y * 4, depth_c * 4)
    )
    return (flattened, hidden, fine_out)


def materials(fine_out):
    wave_speed = 0.15 + 0.25 * jax.nn.sigmoid(fine_out[0])
    density = 1.0 + 1.5 * jax.nn.sigmoid(fine_out[1])
    return (density * wave_speed * wave_speed, 1.0 / density)


def decoder_grads(flattened, hidden, fine_out, grad_mod, grad_buoy, w_first, w_second):
    sig_speed = jax.nn.sigmoid(fine_out[0])
    sig_dens = jax.nn.sigmoid(fine_out[1])
    wave_speed = 0.15 + 0.25 * sig_speed
    density = 1.0 + 1.5 * sig_dens
    grad_speed = grad_mod * 2.0 * density * wave_speed
    grad_dens = grad_mod * wave_speed * wave_speed - grad_buoy / (density * density)
    grad_fine = jnp.stack(
        [
            grad_speed * 0.25 * sig_speed * (1.0 - sig_speed),
            grad_dens * 1.5 * sig_dens * (1.0 - sig_dens),
        ]
    )
    size_x, size_y, size_z = (grad_fine.shape[1], grad_fine.shape[2], grad_fine.shape[3])
    grad_out = (
        grad_fine.reshape(2, size_x // 4, 4, size_y // 4, 4, size_z // 4, 4)
        .transpose(5, 1, 3, 0, 2, 4, 6)
        .reshape(-1, 128)
    )
    grad_hidden = jnp.dot(grad_out, w_second.T, precision=lax.Precision.HIGHEST)
    grad_pre = grad_hidden * (1.0 - hidden * hidden)
    grad_latent = jnp.dot(grad_pre, w_first.T, precision=lax.Precision.HIGHEST).reshape(
        size_z // 4, size_x // 4, size_y // 4 * CH
    )
    grad_second = jnp.dot(hidden.T, grad_out, precision=lax.Precision.HIGHEST)
    grad_first = jnp.dot(flattened.T, grad_pre, precision=lax.Precision.HIGHEST)
    return (grad_latent, grad_first, grad_second)


RIM = 7
VRIM = 4
PAD = 8


def receiver_kernel(column_ref, depth_ref, parts_ref, hits_ref, recorded_ref, weights_ref):
    count = column_ref.shape[1]
    size_x, size_y, size_z = hits_ref.shape
    deep = (
        lax.broadcasted_iota(jnp.int32, (size_z, count), 0) == depth_ref[...]
    ).astype(jnp.float32)
    weights_ref[pl.ds(0, size_z), :] = deep.astype(jnp.bfloat16)
    for part in range(2 * STEPS):
        weights_ref[pl.ds((part + 1) * size_z, size_z), :] = (
            deep * parts_ref[pl.ds(part, 1), :]
        ).astype(jnp.bfloat16)
    chunk = 8 if size_x % 8 == 0 else 1
    rows = chunk * size_y

    def planes(step, carry):
        index = lax.broadcasted_iota(jnp.int32, (rows, count), 0) + step * rows
        picks = (index == column_ref[...]).astype(jnp.float32).astype(jnp.bfloat16)
        summed = lax.dot_general(
            picks, weights_ref[...], (((1,), (1,)), ((), ())), preferred_element_type=jnp.float32
        ).reshape(chunk, size_y, (2 * STEPS + 1) * size_z)
        here = pl.ds(step * chunk, chunk)
        hits_ref[here] = summed[:, :, :size_z]
        for moment in range(STEPS):
            first = (1 + 2 * moment) * size_z
            recorded_ref[moment, here] = (
                summed[:, :, first : first + size_z]
                + summed[:, :, first + size_z : first + 2 * size_z]
            )
        return carry

    lax.fori_loop(0, size_x // chunk, planes, 0)


def receiver_fields(receivers, observed_now, anchor_x, anchor_y, shape):
    size_x, size_y, size_z = shape
    local_x = receivers[0] - anchor_x
    local_y = receivers[1] - anchor_y
    inside = (local_x >= 0) & (local_x < size_x) & (local_y >= 0) & (local_y < size_y)
    column = jnp.where(inside, local_x * size_y + local_y, -1)
    count = column.shape[0]
    high = lax.reduce_precision(observed_now, 8, 7)
    low = lax.reduce_precision(observed_now - high, 8, 7)
    parts = jnp.stack([high, low], axis=1).reshape(2 * STEPS, count)
    return pl.pallas_call(
        receiver_kernel,
        out_shape=(
            jax.ShapeDtypeStruct(shape, jnp.float32),
            jax.ShapeDtypeStruct((STEPS,) + shape, jnp.float32),
        ),
        scratch_shapes=[pltpu.VMEM(((2 * STEPS + 1) * size_z, count), jnp.bfloat16)],
        compiler_params=pltpu.CompilerParams(vmem_limit_bytes=40 * 1024 * 1024),
        cost_estimate=pl.CostEstimate(
            flops=2 * size_x * size_y * count * 7 * size_z,
            bytes_accessed=16 * size_x * size_y * size_z,
            transcendentals=0,
        ),
    )(column[None, :], receivers[2][None, :], parts)


def window_kernel(
    place_ref,
    amp_ref,
    dplus_ref,
    dminus_ref,
    mod_ref,
    buoy_ref,
    fwd_press,
    fwd_vel,
    adj_press,
    adj_vel,
    hits_ref,
    recorded_ref,
    out_ref,
    press,
    buoy,
    vel_x,
    vel_y,
    vel_z,
    diverge_z,
    misfit,
    div_at,
    slope_x,
    slope_y,
    slope_z,
    local_sem,
    send_sem,
    recv_sem,
):
    size_x, size_y, size_z = mod_ref.shape
    tall = size_y + 2 * PAD
    mid_y = pl.ds(PAD, size_y)
    me_x, me_y = lax.axis_index("gx"), lax.axis_index("gy")
    has = (
        me_x > 0,
        me_x < lax.axis_size("gx") - 1,
        me_y > 0,
        me_y < lax.axis_size("gy") - 1,
    )
    target = ({"gx": me_x - 1}, {"gx": me_x + 1}, {"gy": me_y - 1}, {"gy": me_y + 1})

    barrier = pltpu.get_barrier_semaphore()
    for side in range(4):

        @pl.when(has[side])
        def _():
            pl.semaphore_signal(
                barrier, inc=1, device_id=target[side], device_id_type=pl.DeviceIdType.MESH
            )

    loads = [
        (fwd_press, press.at[0, pl.ds(RIM, size_x), mid_y]),
        (buoy_ref, buoy.at[pl.ds(VRIM, size_x), mid_y]),
    ]
    for way, vel in enumerate((fwd_vel, adj_vel)):
        loads.append((vel.at[0], vel_x.at[way, pl.ds(VRIM, size_x)]))
        loads.append((vel.at[1], vel_y.at[way, :, mid_y]))
        loads.append((vel.at[2], vel_z.at[way]))
    moves = [
        pltpu.make_async_copy(source, dest, local_sem.at[n])
        for n, (source, dest) in enumerate(loads)
    ]
    for move in moves:
        move.start()

    def channel(slot, pairs):
        return [
            pltpu.make_async_remote_copy(
                src_ref=pairs[side][0],
                dst_ref=pairs[side][1],
                send_sem=send_sem.at[slot, side],
                recv_sem=recv_sem.at[slot, side ^ 1],
                device_id=target[side],
                device_id_type=pl.DeviceIdType.MESH,
            )
            for side in range(4)
        ]

    def press_pairs(state, edges):
        low_x, high_x = pl.ds(0, RIM), pl.ds(size_x + RIM, RIM)
        low_y, high_y = pl.ds(0, PAD), pl.ds(size_y + PAD, PAD)
        mid_x = pl.ds(RIM, size_x)
        return [
            (edges[0], press.at[state, high_x, mid_y]),
            (edges[1], press.at[state, low_x, mid_y]),
            (edges[2], press.at[state, mid_x, high_y]),
            (edges[3], press.at[state, mid_x, low_y]),
        ]

    def own_edges(state):
        mid_x = pl.ds(RIM, size_x)
        return [
            press.at[state, pl.ds(RIM, RIM), mid_y],
            press.at[state, pl.ds(size_x, RIM), mid_y],
            press.at[state, mid_x, pl.ds(PAD, PAD)],
            press.at[state, mid_x, pl.ds(size_y, PAD)],
        ]

    first_edges = [
        fwd_press.at[pl.ds(0, RIM)],
        fwd_press.at[pl.ds(size_x - RIM, RIM)],
        fwd_press.at[:, pl.ds(0, PAD)],
        fwd_press.at[:, pl.ds(size_y - PAD, PAD)],
    ]
    channels = [channel(0, press_pairs(0, first_edges))]
    for state in range(1, 2 * STEPS):
        channels.append(channel(state, press_pairs(state, own_edges(state))))
    for way, vel in enumerate((fwd_vel, adj_vel)):
        channels.append(
            channel(
                2 * STEPS + way,
                [
                    (vel.at[0, pl.ds(0, VRIM)], vel_x.at[way, pl.ds(size_x + VRIM, VRIM)]),
                    (vel.at[0, pl.ds(size_x - VRIM, VRIM)], vel_x.at[way, pl.ds(0, VRIM)]),
                    (vel.at[1, :, pl.ds(0, PAD)], vel_y.at[way, :, pl.ds(size_y + PAD, PAD)]),
                    (vel.at[1, :, pl.ds(size_y - PAD, PAD)], vel_y.at[way, :, pl.ds(0, PAD)]),
                ],
            )
        )
    mid_v = pl.ds(VRIM, size_x)
    channels.append(
        channel(
            2 * STEPS + 2,
            [
                (buoy_ref.at[pl.ds(0, VRIM)], buoy.at[pl.ds(size_x + VRIM, VRIM), mid_y]),
                (buoy_ref.at[pl.ds(size_x - VRIM, VRIM)], buoy.at[pl.ds(0, VRIM), mid_y]),
                (buoy_ref.at[:, pl.ds(0, PAD)], buoy.at[mid_v, pl.ds(size_y + PAD, PAD)]),
                (buoy_ref.at[:, pl.ds(size_y - PAD, PAD)], buoy.at[mid_v, pl.ds(0, PAD)]),
            ],
        )
    )

    def send(slot, sides):
        for side in sides:

            @pl.when(has[side])
            def _():
                channels[slot][side].start()

    def receive(slot):
        for side in range(4):

            @pl.when(has[side])
            def _():
                channels[slot][side ^ 1].wait_recv()

    def sent(slot):
        for side in range(4):

            @pl.when(has[side])
            def _():
                channels[slot][side].wait_send()

    for side in range(4):

        @pl.when(jnp.logical_not(has[side]))
        def _():
            far = side % 2
            if side < 2:
                rows = pl.ds(far * (size_x + RIM), RIM)
                vrows = pl.ds(far * (size_x + VRIM), VRIM)
                for state in range(2 * STEPS):
                    press[state, rows, mid_y] = jnp.zeros((RIM, size_y, size_z), jnp.float32)
                buoy[vrows, mid_y] = jnp.zeros((VRIM, size_y, size_z), jnp.float32)
                for way in range(2):
                    vel_x[way, vrows] = jnp.zeros((VRIM, size_y, size_z), jnp.float32)
            else:
                cols = pl.ds(far * (size_y + PAD), PAD)
                blank = jnp.zeros((size_x, PAD, size_z), jnp.float32)
                for state in range(2 * STEPS):
                    press[state, pl.ds(RIM, size_x), cols] = blank
                buoy[mid_v, cols] = blank
                for way in range(2):
                    vel_y[way, :, cols] = blank

    peers = sum(jnp.where(here, 1, 0) for here in has)
    pl.semaphore_wait(barrier, peers)

    every = range(4)
    send(0, every)
    send(2 * STEPS + 2, every)
    send(2 * STEPS, every)
    send(2 * STEPS + 1, every)
    for move in moves:
        move.wait()

    src_x, src_y, src_z = place_ref[0], place_ref[1], place_ref[2]
    at_source = (
        (lax.broadcasted_iota(jnp.int32, (size_y, size_z), 0) == src_y)
        & (lax.broadcasted_iota(jnp.int32, (size_y, size_z), 1) == src_z)
    ).astype(jnp.float32)
    chunk = 8 if size_x % 8 == 0 else 1
    exact = lax.Precision.HIGHEST

    def step(state, way, moment):
        def depth_part(turn, carry):
            here = pl.ds(turn * chunk, chunk)
            inner = press[state, pl.ds(turn * chunk + RIM, chunk), mid_y]
            slope = jnp.dot(
                inner.reshape(chunk * size_y, size_z), dplus_ref[...], precision=exact
            ).reshape(inner.shape)
            if way == 0:
                slope_z[moment, here] = slope
            moved = vel_z[way, here] - buoy_ref_in(turn) * slope
            vel_z[way, here] = moved
            diverge_z[here] = jnp.dot(
                moved.reshape(chunk * size_y, size_z), dminus_ref[...], precision=exact
            ).reshape(inner.shape)
            return carry

        def buoy_ref_in(turn):
            return buoy[pl.ds(turn * chunk + VRIM, chunk), mid_y]

        lax.fori_loop(0, size_x // chunk, depth_part, 0)

        if state == 0:
            receive(2 * STEPS + 2)
        if state % STEPS == 0:
            receive(2 * STEPS + way)
        receive(state)

        def along_x(i):
            slope = 0.0
            for order, weight in enumerate(coeffs):
                r = order + 1
                slope = slope + weight * (
                    press[state, i + VRIM - 1 + r, mid_y] - press[state, i + VRIM - r, mid_y]
                )
            vel_x[way, i] = vel_x[way, i] - buoy[i, mid_y] * slope
            return slope

        def ghost_low(i, carry):
            along_x(i)
            return carry

        def faces(x, carry):
            slope = along_x(x + VRIM)
            plane = press[state, x + RIM]
            slope_b = 0.0
            for order, weight in enumerate(coeffs):
                r = order + 1
                back = plane if r == 1 else pltpu.roll(plane, r - 1, 0)
                slope_b = slope_b + weight * (pltpu.roll(plane, tall - r, 0) - back)
            vel_y[way, x] = vel_y[way, x] - buoy[x + VRIM] * slope_b
            if way == 0:
                slope_x[moment, x] = slope
                slope_y[moment, x] = slope_b[PAD : PAD + size_y]
            return carry

        lax.fori_loop(0, VRIM, ghost_low, 0)
        lax.fori_loop(size_x + VRIM, size_x + 2 * VRIM - 1, ghost_low, 0)
        lax.fori_loop(0, size_x, faces, 0)

        def finish(k, carry):
            x = lax.rem(k + size_x - RIM, size_x)
            plane = vel_y[way, x]
            div = diverge_z[x]
            across = 0.0
            for order, weight in enumerate(coeffs):
                r = order + 1
                ahead = plane if r == 1 else pltpu.roll(plane, tall - r + 1, 0)
                across = across + weight * (ahead - pltpu.roll(plane, r, 0))
                div = div + weight * (
                    vel_x[way, x + VRIM + r - 1] - vel_x[way, x + VRIM - r]
                )
            div = div + across[PAD : PAD + size_y]
            value = press[state, x + RIM, mid_y] - mod_ref[x] * div
            if way == 0:
                value = value + at_source * jnp.where(x == src_x, amp_ref[moment], 0.0)
                residue = hits_ref[x] * value - recorded_ref[moment, x]
                div_at[moment, x] = div
                if moment == STEPS - 1:
                    press[state + 1, x + RIM, mid_y] = adj_press[x] + residue
                else:
                    misfit[moment, x] = residue
                    press[state + 1, x + RIM, mid_y] = value
            else:
                part_mod = value * div_at[moment, x]
                part_buoy = (
                    vel_x[way, x + VRIM] * slope_x[moment, x]
                    + plane[PAD : PAD + size_y] * slope_y[moment, x]
                    + vel_z[way, x] * slope_z[moment, x]
                )
                if moment == STEPS - 1:
                    out_ref[0, x] = -part_mod
                    out_ref[1, x] = -part_buoy
                else:
                    out_ref[0, x] = out_ref[0, x] - part_mod
                    out_ref[1, x] = out_ref[1, x] - part_buoy
                if moment > 0:
                    press[state + 1, x + RIM, mid_y] = value + misfit[moment - 1, x]
            return carry

        edge = min(2 * RIM, size_x)
        lax.fori_loop(0, edge, finish, 0)
        more = state + 1 < 2 * STEPS
        if more:
            send(state + 1, (0, 1))
        lax.fori_loop(edge, size_x, finish, 0)
        if more:
            send(state + 1, (2, 3))

    for moment in range(STEPS):
        step(moment, 0, moment)
    for turn in range(STEPS):
        step(STEPS + turn, 1, STEPS - 1 - turn)
    for slot in range(2 * STEPS + 3):
        sent(slot)


def depth_matrices(size_z):
    source = lax.broadcasted_iota(jnp.int32, (size_z, size_z), 0)
    dest = lax.broadcasted_iota(jnp.int32, (size_z, size_z), 1)
    plus = jnp.zeros((size_z, size_z), jnp.float32)
    minus = plus
    for order, weight in enumerate(coeffs):
        r = order + 1
        plus = plus + jnp.where(source == dest + r, weight, 0.0)
        plus = plus - jnp.where(source == dest - r + 1, weight, 0.0)
        minus = minus + jnp.where(source == dest + r - 1, weight, 0.0)
        minus = minus - jnp.where(source == dest - r, weight, 0.0)
    return plus, minus


def window(place, amps, modulus, buoyancy, fwd_press, fwd_vel, adj_press, adj_vel, hits, recorded):
    size_x, size_y, size_z = fwd_press.shape
    tall = size_y + 2 * PAD
    plus, minus = depth_matrices(size_z)
    vmem = pl.BlockSpec(memory_space=pltpu.VMEM)
    smem = pl.BlockSpec(memory_space=pltpu.SMEM)
    field = (size_x, size_y, size_z)

    def scratch(*shape):
        return pltpu.VMEM(shape, jnp.float32)

    slots = 2 * STEPS + 3
    return pl.pallas_call(
        window_kernel,
        out_shape=jax.ShapeDtypeStruct((2,) + field, jnp.float32),
        in_specs=[smem, smem] + [vmem] * 10,
        out_specs=vmem,
        scratch_shapes=[
            scratch(2 * STEPS, size_x + 2 * RIM, tall, size_z),
            scratch(size_x + 2 * VRIM, tall, size_z),
            scratch(2, size_x + 2 * VRIM, size_y, size_z),
            scratch(2, size_x, tall, size_z),
            scratch(2, *field),
            scratch(*field),
            scratch(STEPS - 1, *field),
            scratch(STEPS, *field),
            scratch(STEPS, *field),
            scratch(STEPS, *field),
            scratch(STEPS, *field),
            pltpu.SemaphoreType.DMA((8,)),
            pltpu.SemaphoreType.DMA((slots, 4)),
            pltpu.SemaphoreType.DMA((slots, 4)),
        ],
        compiler_params=pltpu.CompilerParams(
            collective_id=0, has_side_effects=True, vmem_limit_bytes=56 * 1024 * 1024
        ),
    )(place, amps, plus, minus, modulus, buoyancy, fwd_press, fwd_vel, adj_press, adj_vel, hits, recorded)


def body(
    latent,
    w_first,
    w_second,
    fwd_press,
    fwd_vel,
    adj_press,
    adj_vel,
    src_pos,
    src_amp,
    rec_pos,
    observed,
):
    size_x, size_y = (fwd_press.shape[1], fwd_press.shape[2])
    anchor_x = lax.axis_index("gx") * size_x
    anchor_y = lax.axis_index("gy") * size_y
    flattened, hidden, fine_out = decode(latent, w_first, w_second)
    slab_mod, slab_buoy = materials(fine_out)
    stacked = lax.all_gather(jnp.stack([slab_mod, slab_buoy]), "shot", axis=3, tiled=True)
    modulus, buoyancy = (stacked[0], stacked[1])
    hits, recorded = receiver_fields(
        rec_pos[0], observed[0], anchor_x, anchor_y, fwd_press.shape[1:]
    )
    place = jnp.stack([src_pos[0, 0] - anchor_x, src_pos[1, 0] - anchor_y, src_pos[2, 0]])
    totals = window(
        place,
        src_amp[:, 0],
        modulus,
        buoyancy,
        fwd_press[0],
        fwd_vel[0],
        adj_press[0],
        adj_vel[0],
        hits,
        recorded,
    )
    shares = lax.psum_scatter(totals, "shot", scatter_dimension=3, tiled=True)
    grad_latent, grad_first, grad_second = decoder_grads(
        flattened, hidden, fine_out, shares[0], shares[1], w_first, w_second
    )
    grad_first, grad_second = lax.psum((grad_first, grad_second), ("shot", "gx", "gy"))
    return (grad_latent, grad_first, grad_second)


def solution(mesh):
    in_specs = (
        P("shot", "gx", "gy"),
        P(),
        P(),
        P("shot", "gx", "gy", None),
        P("shot", None, "gx", "gy", None),
        P("shot", "gx", "gy", None),
        P("shot", None, "gx", "gy", None),
        P(None, "shot"),
        P(None, "shot"),
        P("shot", None, None),
        P("shot", None, None),
    )
    out_specs = (P("shot", "gx", "gy"), P(), P())
    return jax.shard_map(body, mesh=mesh, in_specs=in_specs, out_specs=out_specs, check_vma=False)
```

```python
import jax
import jax.numpy as jnp
from jax import lax
from jax.experimental import pallas as pl
from jax.experimental.pallas import tpu as pltpu
from jax.sharding import PartitionSpec as P

CH = 64
STEPS = 3


coeffs = (1225.0 / 1024.0, -245.0 / 3072.0, 49.0 / 5120.0, -5.0 / 7168.0)


def axis_peers(axis, distance):
    count = lax.axis_size(axis)
    return {axis: lax.rem(lax.axis_index(axis) + distance, count)}


def greet(axes):
    barrier = pltpu.get_barrier_semaphore()
    total = 0
    for axis in axes:
        for distance in range(1, lax.axis_size(axis)):
            pl.semaphore_signal(
                barrier,
                inc=1,
                device_id=axis_peers(axis, distance),
                device_id_type=pl.DeviceIdType.MESH,
            )
            total += 1
    pl.semaphore_wait(barrier, total)


def to_peer(axis, distance, source, dest, sems, row):
    return pltpu.make_async_remote_copy(
        src_ref=source,
        dst_ref=dest,
        send_sem=sems.at[0, row, distance - 1],
        recv_sem=sems.at[1, row, distance - 1],
        device_id=axis_peers(axis, distance),
        device_id_type=pl.DeviceIdType.MESH,
    )


def gather_kernel(own_ref, out_ref, sems):
    greet(("shot",))
    me = lax.axis_index("shot")
    copies = [
        to_peer("shot", d, own_ref, out_ref.at[me], sems, 0)
        for d in range(1, lax.axis_size("shot"))
    ]
    for copy in copies:
        copy.start()
    out_ref[me] = own_ref[...]
    for copy in copies:
        copy.wait()


def gather_latent(own):
    shots = lax.axis_size("shot")
    vmem = pl.BlockSpec(memory_space=pltpu.VMEM)
    return pl.pallas_call(
        gather_kernel,
        out_shape=jax.ShapeDtypeStruct((shots,) + own.shape, jnp.float32),
        in_specs=[vmem],
        out_specs=vmem,
        scratch_shapes=[pltpu.SemaphoreType.DMA((2, 1, shots - 1))],
        compiler_params=pltpu.CompilerParams(collective_id=1, has_side_effects=True),
    )(own)


def reduce_kernel(share_ref, weight_ref, out_ref, sum_ref, landed, first, second, third, sems):
    greet(("shot", "gx", "gy"))
    me = lax.axis_index("shot")
    copies = []
    for d in range(1, lax.axis_size("shot")):
        there = axis_peers("shot", d)["shot"]
        copies.append(to_peer("shot", d, weight_ref, first.at[me], sems, 0))
        copies.append(to_peer("shot", d, share_ref.at[there], landed.at[me], sems, 1))
    for copy in copies:
        copy.start()
    first[me] = weight_ref[...]
    landed[me] = share_ref[me]

    def total(stack):
        summed = stack[0]
        for n in range(1, stack.shape[0]):
            summed = summed + stack[n]
        return summed

    for copy in copies[::2]:
        copy.wait()
    held, slots, row = first, second, 2
    for axis in ("gx", "gy"):
        mine = lax.axis_index(axis)
        slots[mine] = total(held)
        hops = [
            to_peer(axis, d, slots.at[mine], slots.at[mine], sems, row)
            for d in range(1, lax.axis_size(axis))
        ]
        for hop in hops:
            hop.start()
        if axis == "gx":
            for copy in copies[1::2]:
                copy.wait()
            out_ref[...] = total(landed)
        for hop in hops:
            hop.wait()
        held, slots, row = slots, third, row + 1
    sum_ref[...] = total(held)


def reduce_all(shares, weights):
    sizes = [lax.axis_size(axis) for axis in ("shot", "gx", "gy")]
    vmem = pl.BlockSpec(memory_space=pltpu.VMEM)
    return pl.pallas_call(
        reduce_kernel,
        out_shape=(
            jax.ShapeDtypeStruct(shares.shape[1:], jnp.float32),
            jax.ShapeDtypeStruct(weights.shape, jnp.float32),
        ),
        in_specs=[vmem, vmem],
        out_specs=(vmem, vmem),
        scratch_shapes=[pltpu.VMEM(shares.shape, jnp.float32)]
        + [pltpu.VMEM((size,) + weights.shape, jnp.float32) for size in sizes]
        + [pltpu.SemaphoreType.DMA((2, 4, max(sizes)))],
        compiler_params=pltpu.CompilerParams(collective_id=2, has_side_effects=True),
    )(shares, weights)


exact = lax.Precision.HIGHEST
contract_lanes = (((1,), (1,)), ((), ()))


def by_offset(values_in):
    offset = lax.broadcasted_iota(jnp.int32, values_in.shape, 1) % 4
    return [jnp.where(offset == k, values_in, 0.0) for k in range(4)]


def decode_kernel(wide_ref, first_ref, second_ref, mod_ref, buoy_ref, hidden_ref, fine_ref):
    rows_b, size_z = wide_ref.shape[1], wide_ref.shape[3]

    def row(a, carry):
        latent = jnp.concatenate([wide_ref[a, b] for b in range(rows_b)], axis=1)
        hidden = jnp.tanh(jnp.dot(first_ref[...], latent, precision=exact))
        hidden_ref[a] = hidden
        fine = jnp.dot(
            second_ref[...], jnp.concatenate(by_offset(hidden), axis=0), precision=exact
        )
        fine_ref[a] = fine
        speed = 0.15 + 0.25 * jax.nn.sigmoid(fine[:16])
        density = 1.0 + 1.5 * jax.nn.sigmoid(fine[16:])
        modulus = density * speed * speed
        buoyancy = 1.0 / density
        for i in range(4):
            for b in range(rows_b):
                lanes = slice(b * size_z, (b + 1) * size_z)
                mod_ref[4 * a + i, 4 * b : 4 * b + 4] = modulus[4 * i : 4 * i + 4, lanes]
                buoy_ref[4 * a + i, 4 * b : 4 * b + 4] = buoyancy[4 * i : 4 * i + 4, lanes]
        return carry

    lax.fori_loop(0, wide_ref.shape[0], row, 0)


def decode(wide, w_first, w_second):
    rows_a, rows_b, channels, size_z = wide.shape
    field = jax.ShapeDtypeStruct((4 * rows_a, 4 * rows_b, size_z), jnp.float32)
    lanes = rows_b * size_z
    by_k = w_second.reshape(channels, 32, 4).transpose(1, 2, 0).reshape(32, 4 * channels)
    return pl.pallas_call(
        decode_kernel,
        out_shape=(
            field,
            field,
            jax.ShapeDtypeStruct((rows_a, channels, lanes), jnp.float32),
            jax.ShapeDtypeStruct((rows_a, 32, lanes), jnp.float32),
        ),
        compiler_params=pltpu.CompilerParams(vmem_limit_bytes=40 * 1024 * 1024),
    )(wide, w_first.T, by_k)


def gradient_kernel(
    totals_ref, wide_ref, hidden_ref, fine_ref, first_ref, back_ref, out_ref, gf_ref, gs_ref, mix
):
    rows_b, size_z = wide_ref.shape[1], wide_ref.shape[3]
    gf_ref[...] = jnp.zeros(gf_ref.shape, jnp.float32)
    gs_ref[...] = jnp.zeros(gs_ref.shape, jnp.float32)

    def row(a, carry):
        for field in range(2):
            for i in range(4):
                for b in range(rows_b):
                    top = 16 * field + 4 * i
                    mix[top : top + 4, b * size_z : (b + 1) * size_z] = totals_ref[
                        field, 4 * a + i, 4 * b : 4 * b + 4
                    ]
        grad_mod, grad_buoy = mix[:16], mix[16:]
        sig_speed = jax.nn.sigmoid(fine_ref[a, :16])
        sig_dens = jax.nn.sigmoid(fine_ref[a, 16:])
        speed = 0.15 + 0.25 * sig_speed
        density = 1.0 + 1.5 * sig_dens
        grad_speed = grad_mod * 2.0 * density * speed
        grad_dens = grad_mod * speed * speed - grad_buoy / (density * density)
        grad_fine = jnp.concatenate(
            [
                grad_speed * 0.25 * sig_speed * (1.0 - sig_speed),
                grad_dens * 1.5 * sig_dens * (1.0 - sig_dens),
            ],
            axis=0,
        )
        hidden = hidden_ref[a]
        channels = hidden.shape[0]
        spread = jnp.dot(back_ref[...], grad_fine, precision=exact)
        offset = lax.broadcasted_iota(jnp.int32, hidden.shape, 1) % 4
        grad_hidden = 0.0
        for k in range(4):
            grad_hidden = grad_hidden + jnp.where(
                offset == k, spread[k * channels : (k + 1) * channels], 0.0
            )
        grad_pre = grad_hidden * (1.0 - hidden * hidden)
        grad_wide = jnp.dot(first_ref[...], grad_pre, precision=exact)
        for b in range(rows_b):
            out_ref[a, b] = grad_wide[:, b * size_z : (b + 1) * size_z]
        latent = jnp.concatenate([wide_ref[a, b] for b in range(rows_b)], axis=1)
        gf_ref[...] += lax.dot_general(
            latent, grad_pre, contract_lanes, precision=exact, preferred_element_type=jnp.float32
        )
        gs_ref[...] += lax.dot_general(
            jnp.concatenate(by_offset(hidden), axis=0),
            grad_fine,
            contract_lanes,
            precision=exact,
            preferred_element_type=jnp.float32,
        )
        return carry

    lax.fori_loop(0, wide_ref.shape[0], row, 0)


def decoder_grads(totals, wide, hidden, fine, w_first, w_second):
    rows_a, rows_b, channels, size_z = wide.shape
    back = w_second.reshape(channels, 32, 4).transpose(2, 0, 1).reshape(4 * channels, 32)
    grad_wide, grad_first, by_k = pl.pallas_call(
        gradient_kernel,
        out_shape=(
            jax.ShapeDtypeStruct(wide.shape, jnp.float32),
            jax.ShapeDtypeStruct((channels, channels), jnp.float32),
            jax.ShapeDtypeStruct((4 * channels, 32), jnp.float32),
        ),
        scratch_shapes=[pltpu.VMEM((32, rows_b * size_z), jnp.float32)],
        compiler_params=pltpu.CompilerParams(vmem_limit_bytes=40 * 1024 * 1024),
    )(totals, wide, hidden, fine, w_first, back)
    grad_second = by_k.reshape(4, channels, 32).transpose(1, 2, 0).reshape(channels, 128)
    return grad_wide, grad_first, grad_second


RIM = 7
VRIM = 4
PAD = 8


def receiver_kernel(column_ref, depth_ref, parts_ref, hits_ref, recorded_ref, weights_ref):
    count = column_ref.shape[1]
    size_x, size_y, size_z = hits_ref.shape
    deep = (
        lax.broadcasted_iota(jnp.int32, (size_z, count), 0) == depth_ref[...]
    ).astype(jnp.float32)
    weights_ref[pl.ds(0, size_z), :] = deep.astype(jnp.bfloat16)
    for part in range(2 * STEPS):
        weights_ref[pl.ds((part + 1) * size_z, size_z), :] = (
            deep * parts_ref[pl.ds(part, 1), :]
        ).astype(jnp.bfloat16)
    chunk = 8 if size_x % 8 == 0 else 1
    rows = chunk * size_y

    def planes(step, carry):
        index = lax.broadcasted_iota(jnp.int32, (rows, count), 0) + step * rows
        picks = (index == column_ref[...]).astype(jnp.float32).astype(jnp.bfloat16)
        summed = lax.dot_general(
            picks, weights_ref[...], (((1,), (1,)), ((), ())), preferred_element_type=jnp.float32
        ).reshape(chunk, size_y, (2 * STEPS + 1) * size_z)
        here = pl.ds(step * chunk, chunk)
        hits_ref[here] = summed[:, :, :size_z]
        for moment in range(STEPS):
            first = (1 + 2 * moment) * size_z
            recorded_ref[moment, here] = (
                summed[:, :, first : first + size_z]
                + summed[:, :, first + size_z : first + 2 * size_z]
            )
        return carry

    lax.fori_loop(0, size_x // chunk, planes, 0)


def receiver_fields(receivers, observed_now, anchor_x, anchor_y, shape):
    size_x, size_y, size_z = shape
    local_x = receivers[0] - anchor_x
    local_y = receivers[1] - anchor_y
    inside = (local_x >= 0) & (local_x < size_x) & (local_y >= 0) & (local_y < size_y)
    column = jnp.where(inside, local_x * size_y + local_y, -1)
    count = column.shape[0]
    high = lax.reduce_precision(observed_now, 8, 7)
    low = lax.reduce_precision(observed_now - high, 8, 7)
    parts = jnp.stack([high, low], axis=1).reshape(2 * STEPS, count)
    return pl.pallas_call(
        receiver_kernel,
        out_shape=(
            jax.ShapeDtypeStruct(shape, jnp.float32),
            jax.ShapeDtypeStruct((STEPS,) + shape, jnp.float32),
        ),
        scratch_shapes=[pltpu.VMEM(((2 * STEPS + 1) * size_z, count), jnp.bfloat16)],
        compiler_params=pltpu.CompilerParams(vmem_limit_bytes=40 * 1024 * 1024),
        cost_estimate=pl.CostEstimate(
            flops=2 * size_x * size_y * count * 7 * size_z,
            bytes_accessed=16 * size_x * size_y * size_z,
            transcendentals=0,
        ),
    )(column[None, :], receivers[2][None, :], parts)


def window_kernel(
    place_ref,
    amp_ref,
    dplus_ref,
    dminus_ref,
    mod_ref,
    buoy_ref,
    fwd_press,
    fwd_vel,
    adj_press,
    adj_vel,
    hits_ref,
    recorded_ref,
    out_ref,
    press,
    buoy,
    vel_x,
    vel_y,
    vel_z,
    diverge_z,
    misfit,
    div_at,
    slope_x,
    slope_y,
    slope_z,
    local_sem,
    send_sem,
    recv_sem,
):
    size_x, size_y, size_z = mod_ref.shape
    tall = size_y + 2 * PAD
    mid_y = pl.ds(PAD, size_y)
    me_x, me_y = lax.axis_index("gx"), lax.axis_index("gy")
    has = (
        me_x > 0,
        me_x < lax.axis_size("gx") - 1,
        me_y > 0,
        me_y < lax.axis_size("gy") - 1,
    )
    target = ({"gx": me_x - 1}, {"gx": me_x + 1}, {"gy": me_y - 1}, {"gy": me_y + 1})

    barrier = pltpu.get_barrier_semaphore()
    for side in range(4):

        @pl.when(has[side])
        def _():
            pl.semaphore_signal(
                barrier, inc=1, device_id=target[side], device_id_type=pl.DeviceIdType.MESH
            )

    loads = [
        (fwd_press, press.at[0, pl.ds(RIM, size_x), mid_y]),
        (buoy_ref, buoy.at[pl.ds(VRIM, size_x), mid_y]),
    ]
    for way, vel in enumerate((fwd_vel, adj_vel)):
        loads.append((vel.at[0], vel_x.at[way, pl.ds(VRIM, size_x)]))
        loads.append((vel.at[1], vel_y.at[way, :, mid_y]))
        loads.append((vel.at[2], vel_z.at[way]))
    moves = [
        pltpu.make_async_copy(source, dest, local_sem.at[n])
        for n, (source, dest) in enumerate(loads)
    ]
    for move in moves:
        move.start()

    def channel(slot, pairs):
        return [
            pltpu.make_async_remote_copy(
                src_ref=pairs[side][0],
                dst_ref=pairs[side][1],
                send_sem=send_sem.at[slot, side],
                recv_sem=recv_sem.at[slot, side ^ 1],
                device_id=target[side],
                device_id_type=pl.DeviceIdType.MESH,
            )
            for side in range(4)
        ]

    def press_pairs(state, edges):
        low_x, high_x = pl.ds(0, RIM), pl.ds(size_x + RIM, RIM)
        low_y, high_y = pl.ds(0, PAD), pl.ds(size_y + PAD, PAD)
        mid_x = pl.ds(RIM, size_x)
        return [
            (edges[0], press.at[state, high_x, mid_y]),
            (edges[1], press.at[state, low_x, mid_y]),
            (edges[2], press.at[state, mid_x, high_y]),
            (edges[3], press.at[state, mid_x, low_y]),
        ]

    def own_edges(state):
        mid_x = pl.ds(RIM, size_x)
        return [
            press.at[state, pl.ds(RIM, RIM), mid_y],
            press.at[state, pl.ds(size_x, RIM), mid_y],
            press.at[state, mid_x, pl.ds(PAD, PAD)],
            press.at[state, mid_x, pl.ds(size_y, PAD)],
        ]

    first_edges = [
        fwd_press.at[pl.ds(0, RIM)],
        fwd_press.at[pl.ds(size_x - RIM, RIM)],
        fwd_press.at[:, pl.ds(0, PAD)],
        fwd_press.at[:, pl.ds(size_y - PAD, PAD)],
    ]
    channels = [channel(0, press_pairs(0, first_edges))]
    for state in range(1, 2 * STEPS):
        channels.append(channel(state, press_pairs(state, own_edges(state))))
    for way, vel in enumerate((fwd_vel, adj_vel)):
        channels.append(
            channel(
                2 * STEPS + way,
                [
                    (vel.at[0, pl.ds(0, VRIM)], vel_x.at[way, pl.ds(size_x + VRIM, VRIM)]),
                    (vel.at[0, pl.ds(size_x - VRIM, VRIM)], vel_x.at[way, pl.ds(0, VRIM)]),
                    (vel.at[1, :, pl.ds(0, PAD)], vel_y.at[way, :, pl.ds(size_y + PAD, PAD)]),
                    (vel.at[1, :, pl.ds(size_y - PAD, PAD)], vel_y.at[way, :, pl.ds(0, PAD)]),
                ],
            )
        )
    mid_v = pl.ds(VRIM, size_x)
    channels.append(
        channel(
            2 * STEPS + 2,
            [
                (buoy_ref.at[pl.ds(0, VRIM)], buoy.at[pl.ds(size_x + VRIM, VRIM), mid_y]),
                (buoy_ref.at[pl.ds(size_x - VRIM, VRIM)], buoy.at[pl.ds(0, VRIM), mid_y]),
                (buoy_ref.at[:, pl.ds(0, PAD)], buoy.at[mid_v, pl.ds(size_y + PAD, PAD)]),
                (buoy_ref.at[:, pl.ds(size_y - PAD, PAD)], buoy.at[mid_v, pl.ds(0, PAD)]),
            ],
        )
    )

    def send(slot, sides):
        for side in sides:

            @pl.when(has[side])
            def _():
                channels[slot][side].start()

    def receive(slot):
        for side in range(4):

            @pl.when(has[side])
            def _():
                channels[slot][side ^ 1].wait_recv()

    def sent(slot):
        for side in range(4):

            @pl.when(has[side])
            def _():
                channels[slot][side].wait_send()

    for side in range(4):

        @pl.when(jnp.logical_not(has[side]))
        def _():
            far = side % 2
            if side < 2:
                rows = pl.ds(far * (size_x + RIM), RIM)
                vrows = pl.ds(far * (size_x + VRIM), VRIM)
                for state in range(2 * STEPS):
                    press[state, rows, mid_y] = jnp.zeros((RIM, size_y, size_z), jnp.float32)
                buoy[vrows, mid_y] = jnp.zeros((VRIM, size_y, size_z), jnp.float32)
                for way in range(2):
                    vel_x[way, vrows] = jnp.zeros((VRIM, size_y, size_z), jnp.float32)
            else:
                cols = pl.ds(far * (size_y + PAD), PAD)
                blank = jnp.zeros((size_x, PAD, size_z), jnp.float32)
                for state in range(2 * STEPS):
                    press[state, pl.ds(RIM, size_x), cols] = blank
                buoy[mid_v, cols] = blank
                for way in range(2):
                    vel_y[way, :, cols] = blank

    peers = sum(jnp.where(here, 1, 0) for here in has)
    pl.semaphore_wait(barrier, peers)

    every = range(4)
    send(0, every)
    send(2 * STEPS + 2, every)
    send(2 * STEPS, every)
    send(2 * STEPS + 1, every)
    for move in moves:
        move.wait()

    src_x, src_y, src_z = place_ref[0], place_ref[1], place_ref[2]
    at_source = (
        (lax.broadcasted_iota(jnp.int32, (size_y, size_z), 0) == src_y)
        & (lax.broadcasted_iota(jnp.int32, (size_y, size_z), 1) == src_z)
    ).astype(jnp.float32)
    chunk = 8 if size_x % 8 == 0 else 1
    def step(state, way, moment):
        def depth_part(turn, carry):
            here = pl.ds(turn * chunk, chunk)
            inner = press[state, pl.ds(turn * chunk + RIM, chunk), mid_y]
            slope = jnp.dot(
                inner.reshape(chunk * size_y, size_z), dplus_ref[...], precision=exact
            ).reshape(inner.shape)
            if way == 0:
                slope_z[moment, here] = slope
            moved = vel_z[way, here] - buoy_ref_in(turn) * slope
            vel_z[way, here] = moved
            diverge_z[here] = jnp.dot(
                moved.reshape(chunk * size_y, size_z), dminus_ref[...], precision=exact
            ).reshape(inner.shape)
            return carry

        def buoy_ref_in(turn):
            return buoy[pl.ds(turn * chunk + VRIM, chunk), mid_y]

        lax.fori_loop(0, size_x // chunk, depth_part, 0)

        if state == 0:
            receive(2 * STEPS + 2)
        if state % STEPS == 0:
            receive(2 * STEPS + way)
        receive(state)

        def along_x(i):
            slope = 0.0
            for order, weight in enumerate(coeffs):
                r = order + 1
                slope = slope + weight * (
                    press[state, i + VRIM - 1 + r, mid_y] - press[state, i + VRIM - r, mid_y]
                )
            vel_x[way, i] = vel_x[way, i] - buoy[i, mid_y] * slope
            return slope

        def ghost_low(i, carry):
            along_x(i)
            return carry

        def faces(x, carry):
            slope = along_x(x + VRIM)
            plane = press[state, x + RIM]
            slope_b = 0.0
            for order, weight in enumerate(coeffs):
                r = order + 1
                back = plane if r == 1 else pltpu.roll(plane, r - 1, 0)
                slope_b = slope_b + weight * (pltpu.roll(plane, tall - r, 0) - back)
            vel_y[way, x] = vel_y[way, x] - buoy[x + VRIM] * slope_b
            if way == 0:
                slope_x[moment, x] = slope
                slope_y[moment, x] = slope_b[PAD : PAD + size_y]
            return carry

        lax.fori_loop(0, VRIM, ghost_low, 0)
        lax.fori_loop(size_x + VRIM, size_x + 2 * VRIM - 1, ghost_low, 0)
        lax.fori_loop(0, size_x, faces, 0)

        def finish(k, carry):
            x = lax.rem(k + size_x - RIM, size_x)
            plane = vel_y[way, x]
            div = diverge_z[x]
            across = 0.0
            for order, weight in enumerate(coeffs):
                r = order + 1
                ahead = plane if r == 1 else pltpu.roll(plane, tall - r + 1, 0)
                across = across + weight * (ahead - pltpu.roll(plane, r, 0))
                div = div + weight * (
                    vel_x[way, x + VRIM + r - 1] - vel_x[way, x + VRIM - r]
                )
            div = div + across[PAD : PAD + size_y]
            value = press[state, x + RIM, mid_y] - mod_ref[x] * div
            if way == 0:
                value = value + at_source * jnp.where(x == src_x, amp_ref[moment], 0.0)
                residue = hits_ref[x] * value - recorded_ref[moment, x]
                div_at[moment, x] = div
                if moment == STEPS - 1:
                    press[state + 1, x + RIM, mid_y] = adj_press[x] + residue
                else:
                    misfit[moment, x] = residue
                    press[state + 1, x + RIM, mid_y] = value
            else:
                part_mod = value * div_at[moment, x]
                part_buoy = (
                    vel_x[way, x + VRIM] * slope_x[moment, x]
                    + plane[PAD : PAD + size_y] * slope_y[moment, x]
                    + vel_z[way, x] * slope_z[moment, x]
                )
                if moment == STEPS - 1:
                    out_ref[0, x] = -part_mod
                    out_ref[1, x] = -part_buoy
                else:
                    out_ref[0, x] = out_ref[0, x] - part_mod
                    out_ref[1, x] = out_ref[1, x] - part_buoy
                if moment > 0:
                    press[state + 1, x + RIM, mid_y] = value + misfit[moment - 1, x]
            return carry

        edge = min(2 * RIM, size_x)
        lax.fori_loop(0, edge, finish, 0)
        more = state + 1 < 2 * STEPS
        if more:
            send(state + 1, (0, 1))
        lax.fori_loop(edge, size_x, finish, 0)
        if more:
            send(state + 1, (2, 3))

    for moment in range(STEPS):
        step(moment, 0, moment)
    for turn in range(STEPS):
        step(STEPS + turn, 1, STEPS - 1 - turn)
    for slot in range(2 * STEPS + 3):
        sent(slot)


def depth_matrices(size_z):
    source = lax.broadcasted_iota(jnp.int32, (size_z, size_z), 0)
    dest = lax.broadcasted_iota(jnp.int32, (size_z, size_z), 1)
    plus = jnp.zeros((size_z, size_z), jnp.float32)
    minus = plus
    for order, weight in enumerate(coeffs):
        r = order + 1
        plus = plus + jnp.where(source == dest + r, weight, 0.0)
        plus = plus - jnp.where(source == dest - r + 1, weight, 0.0)
        minus = minus + jnp.where(source == dest + r - 1, weight, 0.0)
        minus = minus - jnp.where(source == dest - r, weight, 0.0)
    return plus, minus


def window(place, amps, modulus, buoyancy, fwd_press, fwd_vel, adj_press, adj_vel, hits, recorded):
    size_x, size_y, size_z = fwd_press.shape
    tall = size_y + 2 * PAD
    plus, minus = depth_matrices(size_z)
    vmem = pl.BlockSpec(memory_space=pltpu.VMEM)
    smem = pl.BlockSpec(memory_space=pltpu.SMEM)
    field = (size_x, size_y, size_z)

    def scratch(*shape):
        return pltpu.VMEM(shape, jnp.float32)

    slots = 2 * STEPS + 3
    return pl.pallas_call(
        window_kernel,
        out_shape=jax.ShapeDtypeStruct((2,) + field, jnp.float32),
        in_specs=[smem, smem] + [vmem] * 10,
        out_specs=vmem,
        scratch_shapes=[
            scratch(2 * STEPS, size_x + 2 * RIM, tall, size_z),
            scratch(size_x + 2 * VRIM, tall, size_z),
            scratch(2, size_x + 2 * VRIM, size_y, size_z),
            scratch(2, size_x, tall, size_z),
            scratch(2, *field),
            scratch(*field),
            scratch(STEPS - 1, *field),
            scratch(STEPS, *field),
            scratch(STEPS, *field),
            scratch(STEPS, *field),
            scratch(STEPS, *field),
            pltpu.SemaphoreType.DMA((8,)),
            pltpu.SemaphoreType.DMA((slots, 4)),
            pltpu.SemaphoreType.DMA((slots, 4)),
        ],
        compiler_params=pltpu.CompilerParams(
            collective_id=0, has_side_effects=True, vmem_limit_bytes=56 * 1024 * 1024
        ),
    )(place, amps, plus, minus, modulus, buoyancy, fwd_press, fwd_vel, adj_press, adj_vel, hits, recorded)


def body(
    latent,
    w_first,
    w_second,
    fwd_press,
    fwd_vel,
    adj_press,
    adj_vel,
    src_pos,
    src_amp,
    rec_pos,
    observed,
):
    size_x, size_y = (fwd_press.shape[1], fwd_press.shape[2])
    anchor_x = lax.axis_index("gx") * size_x
    anchor_y = lax.axis_index("gy") * size_y
    depth_c, rows_x, merged = latent.shape
    size_z = fwd_press.shape[3]
    everything = gather_latent(latent.reshape(depth_c, rows_x * merged))
    all_depth = size_z // 4
    repeat = (
        lax.broadcasted_iota(jnp.int32, (all_depth, size_z), 1) // 4
        == lax.broadcasted_iota(jnp.int32, (all_depth, size_z), 0)
    ).astype(jnp.float32)
    wide = lax.dot_general(
        everything.reshape(all_depth, rows_x * merged),
        repeat,
        (((0,), (0,)), ((), ())),
        precision=exact,
    ).reshape(rows_x, merged // CH, CH, size_z)
    modulus, buoyancy, hidden, fine = decode(wide, w_first, w_second)
    hits, recorded = receiver_fields(
        rec_pos[0], observed[0], anchor_x, anchor_y, fwd_press.shape[1:]
    )
    place = jnp.stack([src_pos[0, 0] - anchor_x, src_pos[1, 0] - anchor_y, src_pos[2, 0]])
    totals = window(
        place,
        src_amp[:, 0],
        modulus,
        buoyancy,
        fwd_press[0],
        fwd_vel[0],
        adj_press[0],
        adj_vel[0],
        hits,
        recorded,
    )
    grad_wide, grad_first, grad_second = decoder_grads(
        totals, wide, hidden, fine, w_first, w_second
    )
    grad_depth = lax.dot_general(
        repeat, grad_wide.reshape(rows_x * merged, size_z), contract_lanes, precision=exact
    )
    weights = jnp.concatenate(
        [grad_second, jnp.pad(grad_first, ((0, 0), (0, 128 - CH)))], axis=0
    )
    own, weights = reduce_all(grad_depth.reshape(-1, depth_c, rows_x * merged), weights)
    return (own.reshape(latent.shape), weights[CH:, :CH], weights[:CH])


def solution(mesh):
    in_specs = (
        P("shot", "gx", "gy"),
        P(),
        P(),
        P("shot", "gx", "gy", None),
        P("shot", None, "gx", "gy", None),
        P("shot", "gx", "gy", None),
        P("shot", None, "gx", "gy", None),
        P(None, "shot"),
        P(None, "shot"),
        P("shot", None, None),
        P("shot", None, None),
    )
    out_specs = (P("shot", "gx", "gy"), P(), P())
    return jax.shard_map(body, mesh=mesh, in_specs=in_specs, out_specs=out_specs, check_vma=False)
```

```python
import jax
import jax.numpy as jnp
from jax import lax
from jax.experimental import pallas as pl
from jax.experimental.pallas import tpu as pltpu
from jax.sharding import PartitionSpec as P

CH = 64
STEPS = 3


coeffs = (1225.0 / 1024.0, -245.0 / 3072.0, 49.0 / 5120.0, -5.0 / 7168.0)


def axis_peers(axis, distance):
    count = lax.axis_size(axis)
    return {axis: lax.rem(lax.axis_index(axis) + distance, count)}


def greet(axes):
    barrier = pltpu.get_barrier_semaphore()
    total = 0
    for axis in axes:
        for distance in range(1, lax.axis_size(axis)):
            pl.semaphore_signal(
                barrier,
                inc=1,
                device_id=axis_peers(axis, distance),
                device_id_type=pl.DeviceIdType.MESH,
            )
            total += 1
    pl.semaphore_wait(barrier, total)


def to_peer(axis, distance, source, dest, sems, row):
    return pltpu.make_async_remote_copy(
        src_ref=source,
        dst_ref=dest,
        send_sem=sems.at[0, row, distance - 1],
        recv_sem=sems.at[1, row, distance - 1],
        device_id=axis_peers(axis, distance),
        device_id_type=pl.DeviceIdType.MESH,
    )


def gather_kernel(own_ref, out_ref, sems):
    greet(("shot",))
    me = lax.axis_index("shot")
    copies = [
        to_peer("shot", d, own_ref, out_ref.at[me], sems, 0)
        for d in range(1, lax.axis_size("shot"))
    ]
    for copy in copies:
        copy.start()
    out_ref[me] = own_ref[...]
    for copy in copies:
        copy.wait()


def gather_latent(own):
    shots = lax.axis_size("shot")
    vmem = pl.BlockSpec(memory_space=pltpu.VMEM)
    return pl.pallas_call(
        gather_kernel,
        out_shape=jax.ShapeDtypeStruct((shots,) + own.shape, jnp.float32),
        in_specs=[vmem],
        out_specs=vmem,
        scratch_shapes=[pltpu.SemaphoreType.DMA((2, 1, shots - 1))],
        compiler_params=pltpu.CompilerParams(collective_id=1, has_side_effects=True),
    )(own)


def reduce_kernel(share_ref, weight_ref, out_ref, sum_ref, landed, first, second, third, sems):
    greet(("shot", "gx", "gy"))
    me = lax.axis_index("shot")
    copies = []
    for d in range(1, lax.axis_size("shot")):
        there = axis_peers("shot", d)["shot"]
        copies.append(to_peer("shot", d, weight_ref, first.at[me], sems, 0))
        copies.append(to_peer("shot", d, share_ref.at[there], landed.at[me], sems, 1))
    for copy in copies[::2] + copies[1::2]:
        copy.start()
    first[me] = weight_ref[...]
    landed[me] = share_ref[me]

    def total(stack):
        summed = stack[0]
        for n in range(1, stack.shape[0]):
            summed = summed + stack[n]
        return summed

    for copy in copies[::2]:
        copy.wait()
    held, slots, row = first, second, 2
    for axis in ("gx", "gy"):
        mine = lax.axis_index(axis)
        slots[mine] = total(held)
        hops = [
            to_peer(axis, d, slots.at[mine], slots.at[mine], sems, row)
            for d in range(1, lax.axis_size(axis))
        ]
        for hop in hops:
            hop.start()
        if axis == "gx":
            for copy in copies[1::2]:
                copy.wait()
            out_ref[...] = total(landed)
        for hop in hops:
            hop.wait()
        held, slots, row = slots, third, row + 1
    sum_ref[...] = total(held)


def reduce_all(shares, weights):
    sizes = [lax.axis_size(axis) for axis in ("shot", "gx", "gy")]
    vmem = pl.BlockSpec(memory_space=pltpu.VMEM)
    return pl.pallas_call(
        reduce_kernel,
        out_shape=(
            jax.ShapeDtypeStruct(shares.shape[1:], jnp.float32),
            jax.ShapeDtypeStruct(weights.shape, jnp.float32),
        ),
        in_specs=[vmem, vmem],
        out_specs=(vmem, vmem),
        scratch_shapes=[pltpu.VMEM(shares.shape, jnp.float32)]
        + [pltpu.VMEM((size,) + weights.shape, jnp.float32) for size in sizes]
        + [pltpu.SemaphoreType.DMA((2, 4, max(sizes)))],
        compiler_params=pltpu.CompilerParams(collective_id=2, has_side_effects=True),
    )(shares, weights)


exact = lax.Precision.HIGHEST
contract_lanes = (((1,), (1,)), ((), ()))


def by_offset(values_in):
    offset = lax.broadcasted_iota(jnp.int32, values_in.shape, 1) % 4
    return [jnp.where(offset == k, values_in, 0.0) for k in range(4)]


def decode_kernel(wide_ref, first_ref, second_ref, mod_ref, buoy_ref, hidden_ref, fine_ref):
    rows_b, size_z = wide_ref.shape[1], wide_ref.shape[3]

    def row(a, carry):
        latent = jnp.concatenate([wide_ref[a, b] for b in range(rows_b)], axis=1)
        hidden = jnp.tanh(jnp.dot(first_ref[...], latent, precision=exact))
        hidden_ref[a] = hidden
        fine = jnp.dot(
            second_ref[...], jnp.concatenate(by_offset(hidden), axis=0), precision=exact
        )
        fine_ref[a] = fine
        speed = 0.15 + 0.25 * jax.nn.sigmoid(fine[:16])
        density = 1.0 + 1.5 * jax.nn.sigmoid(fine[16:])
        modulus = density * speed * speed
        buoyancy = 1.0 / density
        for i in range(4):
            for b in range(rows_b):
                lanes = slice(b * size_z, (b + 1) * size_z)
                mod_ref[4 * a + i, 4 * b : 4 * b + 4] = modulus[4 * i : 4 * i + 4, lanes]
                buoy_ref[4 * a + i, 4 * b : 4 * b + 4] = buoyancy[4 * i : 4 * i + 4, lanes]
        return carry

    lax.fori_loop(0, wide_ref.shape[0], row, 0)


def decode(wide, w_first, w_second):
    rows_a, rows_b, channels, size_z = wide.shape
    field = jax.ShapeDtypeStruct((4 * rows_a, 4 * rows_b, size_z), jnp.float32)
    lanes = rows_b * size_z
    by_k = w_second.reshape(channels, 32, 4).transpose(1, 2, 0).reshape(32, 4 * channels)
    return pl.pallas_call(
        decode_kernel,
        out_shape=(
            field,
            field,
            jax.ShapeDtypeStruct((rows_a, channels, lanes), jnp.float32),
            jax.ShapeDtypeStruct((rows_a, 32, lanes), jnp.float32),
        ),
        compiler_params=pltpu.CompilerParams(vmem_limit_bytes=40 * 1024 * 1024),
    )(wide, w_first.T, by_k)


def gradient_kernel(
    totals_ref, wide_ref, hidden_ref, fine_ref, first_ref, back_ref, out_ref, gf_ref, gs_ref, mix
):
    rows_b, size_z = wide_ref.shape[1], wide_ref.shape[3]
    gf_ref[...] = jnp.zeros(gf_ref.shape, jnp.float32)
    gs_ref[...] = jnp.zeros(gs_ref.shape, jnp.float32)

    def row(a, carry):
        for field in range(2):
            for i in range(4):
                for b in range(rows_b):
                    top = 16 * field + 4 * i
                    mix[top : top + 4, b * size_z : (b + 1) * size_z] = totals_ref[
                        field, 4 * a + i, 4 * b : 4 * b + 4
                    ]
        grad_mod, grad_buoy = mix[:16], mix[16:]
        sig_speed = jax.nn.sigmoid(fine_ref[a, :16])
        sig_dens = jax.nn.sigmoid(fine_ref[a, 16:])
        speed = 0.15 + 0.25 * sig_speed
        density = 1.0 + 1.5 * sig_dens
        grad_speed = grad_mod * 2.0 * density * speed
        grad_dens = grad_mod * speed * speed - grad_buoy / (density * density)
        grad_fine = jnp.concatenate(
            [
                grad_speed * 0.25 * sig_speed * (1.0 - sig_speed),
                grad_dens * 1.5 * sig_dens * (1.0 - sig_dens),
            ],
            axis=0,
        )
        hidden = hidden_ref[a]
        channels = hidden.shape[0]
        spread = jnp.dot(back_ref[...], grad_fine, precision=exact)
        offset = lax.broadcasted_iota(jnp.int32, hidden.shape, 1) % 4
        grad_hidden = 0.0
        for k in range(4):
            grad_hidden = grad_hidden + jnp.where(
                offset == k, spread[k * channels : (k + 1) * channels], 0.0
            )
        grad_pre = grad_hidden * (1.0 - hidden * hidden)
        grad_wide = jnp.dot(first_ref[...], grad_pre, precision=exact)
        for b in range(rows_b):
            out_ref[a, b] = grad_wide[:, b * size_z : (b + 1) * size_z]
        latent = jnp.concatenate([wide_ref[a, b] for b in range(rows_b)], axis=1)
        gf_ref[...] += lax.dot_general(
            latent, grad_pre, contract_lanes, precision=exact, preferred_element_type=jnp.float32
        )
        gs_ref[...] += lax.dot_general(
            jnp.concatenate(by_offset(hidden), axis=0),
            grad_fine,
            contract_lanes,
            precision=exact,
            preferred_element_type=jnp.float32,
        )
        return carry

    lax.fori_loop(0, wide_ref.shape[0], row, 0)


def decoder_grads(totals, wide, hidden, fine, w_first, w_second):
    rows_a, rows_b, channels, size_z = wide.shape
    back = w_second.reshape(channels, 32, 4).transpose(2, 0, 1).reshape(4 * channels, 32)
    grad_wide, grad_first, by_k = pl.pallas_call(
        gradient_kernel,
        out_shape=(
            jax.ShapeDtypeStruct(wide.shape, jnp.float32),
            jax.ShapeDtypeStruct((channels, channels), jnp.float32),
            jax.ShapeDtypeStruct((4 * channels, 32), jnp.float32),
        ),
        scratch_shapes=[pltpu.VMEM((32, rows_b * size_z), jnp.float32)],
        compiler_params=pltpu.CompilerParams(vmem_limit_bytes=40 * 1024 * 1024),
    )(totals, wide, hidden, fine, w_first, back)
    grad_second = by_k.reshape(4, channels, 32).transpose(1, 2, 0).reshape(channels, 128)
    return grad_wide, grad_first, grad_second


RIM = 7
VRIM = 4
PAD = 8


def receiver_kernel(column_ref, depth_ref, parts_ref, hits_ref, recorded_ref, weights_ref):
    count = column_ref.shape[1]
    size_x, size_y, size_z = hits_ref.shape
    deep = (
        lax.broadcasted_iota(jnp.int32, (size_z, count), 0) == depth_ref[...]
    ).astype(jnp.float32)
    weights_ref[pl.ds(0, size_z), :] = deep.astype(jnp.bfloat16)
    for part in range(2 * STEPS):
        weights_ref[pl.ds((part + 1) * size_z, size_z), :] = (
            deep * parts_ref[pl.ds(part, 1), :]
        ).astype(jnp.bfloat16)
    chunk = 8 if size_x % 8 == 0 else 1
    rows = chunk * size_y

    def planes(step, carry):
        index = lax.broadcasted_iota(jnp.int32, (rows, count), 0) + step * rows
        picks = (index == column_ref[...]).astype(jnp.float32).astype(jnp.bfloat16)
        summed = lax.dot_general(
            picks, weights_ref[...], (((1,), (1,)), ((), ())), preferred_element_type=jnp.float32
        ).reshape(chunk, size_y, (2 * STEPS + 1) * size_z)
        here = pl.ds(step * chunk, chunk)
        hits_ref[here] = summed[:, :, :size_z]
        for moment in range(STEPS):
            first = (1 + 2 * moment) * size_z
            recorded_ref[moment, here] = (
                summed[:, :, first : first + size_z]
                + summed[:, :, first + size_z : first + 2 * size_z]
            )
        return carry

    lax.fori_loop(0, size_x // chunk, planes, 0)


def receiver_fields(receivers, observed_now, anchor_x, anchor_y, shape):
    size_x, size_y, size_z = shape
    local_x = receivers[0] - anchor_x
    local_y = receivers[1] - anchor_y
    inside = (local_x >= 0) & (local_x < size_x) & (local_y >= 0) & (local_y < size_y)
    column = jnp.where(inside, local_x * size_y + local_y, -1)
    count = column.shape[0]
    high = lax.reduce_precision(observed_now, 8, 7)
    low = lax.reduce_precision(observed_now - high, 8, 7)
    parts = jnp.stack([high, low], axis=1).reshape(2 * STEPS, count)
    return pl.pallas_call(
        receiver_kernel,
        out_shape=(
            jax.ShapeDtypeStruct(shape, jnp.float32),
            jax.ShapeDtypeStruct((STEPS,) + shape, jnp.float32),
        ),
        scratch_shapes=[pltpu.VMEM(((2 * STEPS + 1) * size_z, count), jnp.bfloat16)],
        compiler_params=pltpu.CompilerParams(vmem_limit_bytes=40 * 1024 * 1024),
        cost_estimate=pl.CostEstimate(
            flops=2 * size_x * size_y * count * 7 * size_z,
            bytes_accessed=16 * size_x * size_y * size_z,
            transcendentals=0,
        ),
    )(column[None, :], receivers[2][None, :], parts)


def window_kernel(
    place_ref,
    amp_ref,
    dplus_ref,
    dminus_ref,
    mod_ref,
    buoy_ref,
    fwd_press,
    fwd_vel,
    adj_press,
    adj_vel,
    hits_ref,
    recorded_ref,
    out_ref,
    press,
    buoy,
    vel_x,
    vel_y,
    vel_z,
    diverge_z,
    misfit,
    div_at,
    slope_x,
    slope_y,
    slope_z,
    local_sem,
    send_sem,
    recv_sem,
):
    size_x, size_y, size_z = mod_ref.shape
    tall = size_y + 2 * PAD
    mid_y = pl.ds(PAD, size_y)
    me_x, me_y = lax.axis_index("gx"), lax.axis_index("gy")
    has = (
        me_x > 0,
        me_x < lax.axis_size("gx") - 1,
        me_y > 0,
        me_y < lax.axis_size("gy") - 1,
    )
    target = ({"gx": me_x - 1}, {"gx": me_x + 1}, {"gy": me_y - 1}, {"gy": me_y + 1})

    barrier = pltpu.get_barrier_semaphore()
    for side in range(4):

        @pl.when(has[side])
        def _():
            pl.semaphore_signal(
                barrier, inc=1, device_id=target[side], device_id_type=pl.DeviceIdType.MESH
            )

    loads = [
        (fwd_press, press.at[0, pl.ds(RIM, size_x), mid_y]),
        (buoy_ref, buoy.at[pl.ds(VRIM, size_x), mid_y]),
    ]
    for way, vel in enumerate((fwd_vel, adj_vel)):
        loads.append((vel.at[0], vel_x.at[way, pl.ds(VRIM, size_x)]))
        loads.append((vel.at[1], vel_y.at[way, :, mid_y]))
        loads.append((vel.at[2], vel_z.at[way]))
    moves = [
        pltpu.make_async_copy(source, dest, local_sem.at[n])
        for n, (source, dest) in enumerate(loads)
    ]
    for move in moves:
        move.start()

    def channel(slot, pairs):
        return [
            pltpu.make_async_remote_copy(
                src_ref=pairs[side][0],
                dst_ref=pairs[side][1],
                send_sem=send_sem.at[slot, side],
                recv_sem=recv_sem.at[slot, side ^ 1],
                device_id=target[side],
                device_id_type=pl.DeviceIdType.MESH,
            )
            for side in range(4)
        ]

    def press_pairs(state, edges):
        low_x, high_x = pl.ds(0, RIM), pl.ds(size_x + RIM, RIM)
        low_y, high_y = pl.ds(0, PAD), pl.ds(size_y + PAD, PAD)
        mid_x = pl.ds(RIM, size_x)
        return [
            (edges[0], press.at[state, high_x, mid_y]),
            (edges[1], press.at[state, low_x, mid_y]),
            (edges[2], press.at[state, mid_x, high_y]),
            (edges[3], press.at[state, mid_x, low_y]),
        ]

    def own_edges(state):
        mid_x = pl.ds(RIM, size_x)
        return [
            press.at[state, pl.ds(RIM, RIM), mid_y],
            press.at[state, pl.ds(size_x, RIM), mid_y],
            press.at[state, mid_x, pl.ds(PAD, PAD)],
            press.at[state, mid_x, pl.ds(size_y, PAD)],
        ]

    first_edges = [
        fwd_press.at[pl.ds(0, RIM)],
        fwd_press.at[pl.ds(size_x - RIM, RIM)],
        fwd_press.at[:, pl.ds(0, PAD)],
        fwd_press.at[:, pl.ds(size_y - PAD, PAD)],
    ]
    channels = [channel(0, press_pairs(0, first_edges))]
    for state in range(1, 2 * STEPS):
        channels.append(channel(state, press_pairs(state, own_edges(state))))
    for way, vel in enumerate((fwd_vel, adj_vel)):
        channels.append(
            channel(
                2 * STEPS + way,
                [
                    (vel.at[0, pl.ds(0, VRIM)], vel_x.at[way, pl.ds(size_x + VRIM, VRIM)]),
                    (vel.at[0, pl.ds(size_x - VRIM, VRIM)], vel_x.at[way, pl.ds(0, VRIM)]),
                    (vel.at[1, :, pl.ds(0, PAD)], vel_y.at[way, :, pl.ds(size_y + PAD, PAD)]),
                    (vel.at[1, :, pl.ds(size_y - PAD, PAD)], vel_y.at[way, :, pl.ds(0, PAD)]),
                ],
            )
        )
    mid_v = pl.ds(VRIM, size_x)
    channels.append(
        channel(
            2 * STEPS + 2,
            [
                (buoy_ref.at[pl.ds(0, VRIM)], buoy.at[pl.ds(size_x + VRIM, VRIM), mid_y]),
                (buoy_ref.at[pl.ds(size_x - VRIM, VRIM)], buoy.at[pl.ds(0, VRIM), mid_y]),
                (buoy_ref.at[:, pl.ds(0, PAD)], buoy.at[mid_v, pl.ds(size_y + PAD, PAD)]),
                (buoy_ref.at[:, pl.ds(size_y - PAD, PAD)], buoy.at[mid_v, pl.ds(0, PAD)]),
            ],
        )
    )

    def send(slot, sides):
        for side in sides:

            @pl.when(has[side])
            def _():
                channels[slot][side].start()

    def receive(slot):
        for side in range(4):

            @pl.when(has[side])
            def _():
                channels[slot][side ^ 1].wait_recv()

    def sent(slot):
        for side in range(4):

            @pl.when(has[side])
            def _():
                channels[slot][side].wait_send()

    for side in range(4):

        @pl.when(jnp.logical_not(has[side]))
        def _():
            far = side % 2
            if side < 2:
                rows = pl.ds(far * (size_x + RIM), RIM)
                vrows = pl.ds(far * (size_x + VRIM), VRIM)
                for state in range(2 * STEPS):
                    press[state, rows, mid_y] = jnp.zeros((RIM, size_y, size_z), jnp.float32)
                buoy[vrows, mid_y] = jnp.zeros((VRIM, size_y, size_z), jnp.float32)
                for way in range(2):
                    vel_x[way, vrows] = jnp.zeros((VRIM, size_y, size_z), jnp.float32)
            else:
                cols = pl.ds(far * (size_y + PAD), PAD)
                blank = jnp.zeros((size_x, PAD, size_z), jnp.float32)
                for state in range(2 * STEPS):
                    press[state, pl.ds(RIM, size_x), cols] = blank
                buoy[mid_v, cols] = blank
                for way in range(2):
                    vel_y[way, :, cols] = blank

    peers = sum(jnp.where(here, 1, 0) for here in has)
    pl.semaphore_wait(barrier, peers)

    every = range(4)
    send(0, every)
    send(2 * STEPS + 2, every)
    send(2 * STEPS, every)
    send(2 * STEPS + 1, every)
    for move in moves:
        move.wait()

    src_x, src_y, src_z = place_ref[0], place_ref[1], place_ref[2]
    at_source = (
        (lax.broadcasted_iota(jnp.int32, (size_y, size_z), 0) == src_y)
        & (lax.broadcasted_iota(jnp.int32, (size_y, size_z), 1) == src_z)
    ).astype(jnp.float32)
    chunk = 8 if size_x % 8 == 0 else 1
    def step(state, way, moment):
        def depth_part(turn, carry):
            here = pl.ds(turn * chunk, chunk)
            inner = press[state, pl.ds(turn * chunk + RIM, chunk), mid_y]
            slope = jnp.dot(
                inner.reshape(chunk * size_y, size_z), dplus_ref[...], precision=exact
            ).reshape(inner.shape)
            if way == 0:
                slope_z[moment, here] = slope
            moved = vel_z[way, here] - buoy_ref_in(turn) * slope
            vel_z[way, here] = moved
            diverge_z[here] = jnp.dot(
                moved.reshape(chunk * size_y, size_z), dminus_ref[...], precision=exact
            ).reshape(inner.shape)
            return carry

        def buoy_ref_in(turn):
            return buoy[pl.ds(turn * chunk + VRIM, chunk), mid_y]

        lax.fori_loop(0, size_x // chunk, depth_part, 0)

        if state == 0:
            receive(2 * STEPS + 2)
        if state % STEPS == 0:
            receive(2 * STEPS + way)
        receive(state)

        def along_x(i):
            slope = 0.0
            for order, weight in enumerate(coeffs):
                r = order + 1
                slope = slope + weight * (
                    press[state, i + VRIM - 1 + r, mid_y] - press[state, i + VRIM - r, mid_y]
                )
            vel_x[way, i] = vel_x[way, i] - buoy[i, mid_y] * slope
            return slope

        def ghost_low(i, carry):
            along_x(i)
            return carry

        def faces(x, carry):
            slope = along_x(x + VRIM)
            plane = press[state, x + RIM]
            slope_b = 0.0
            for order, weight in enumerate(coeffs):
                r = order + 1
                back = plane if r == 1 else pltpu.roll(plane, r - 1, 0)
                slope_b = slope_b + weight * (pltpu.roll(plane, tall - r, 0) - back)
            vel_y[way, x] = vel_y[way, x] - buoy[x + VRIM] * slope_b
            if way == 0:
                slope_x[moment, x] = slope
                slope_y[moment, x] = slope_b[PAD : PAD + size_y]
            return carry

        lax.fori_loop(0, VRIM, ghost_low, 0)
        lax.fori_loop(size_x + VRIM, size_x + 2 * VRIM - 1, ghost_low, 0)
        lax.fori_loop(0, size_x, faces, 0, unroll=2)

        def finish(k, carry):
            x = lax.rem(k + size_x - RIM, size_x)
            plane = vel_y[way, x]
            div = diverge_z[x]
            across = 0.0
            for order, weight in enumerate(coeffs):
                r = order + 1
                ahead = plane if r == 1 else pltpu.roll(plane, tall - r + 1, 0)
                across = across + weight * (ahead - pltpu.roll(plane, r, 0))
                div = div + weight * (
                    vel_x[way, x + VRIM + r - 1] - vel_x[way, x + VRIM - r]
                )
            div = div + across[PAD : PAD + size_y]
            value = press[state, x + RIM, mid_y] - mod_ref[x] * div
            if way == 0:
                value = value + at_source * jnp.where(x == src_x, amp_ref[moment], 0.0)
                residue = hits_ref[x] * value - recorded_ref[moment, x]
                div_at[moment, x] = div
                if moment == STEPS - 1:
                    press[state + 1, x + RIM, mid_y] = adj_press[x] + residue
                else:
                    misfit[moment, x] = residue
                    press[state + 1, x + RIM, mid_y] = value
            else:
                part_mod = value * div_at[moment, x]
                part_buoy = (
                    vel_x[way, x + VRIM] * slope_x[moment, x]
                    + plane[PAD : PAD + size_y] * slope_y[moment, x]
                    + vel_z[way, x] * slope_z[moment, x]
                )
                if moment == STEPS - 1:
                    out_ref[0, x] = -part_mod
                    out_ref[1, x] = -part_buoy
                else:
                    out_ref[0, x] = out_ref[0, x] - part_mod
                    out_ref[1, x] = out_ref[1, x] - part_buoy
                if moment > 0:
                    press[state + 1, x + RIM, mid_y] = value + misfit[moment - 1, x]
            return carry

        edge = min(2 * RIM, size_x)
        lax.fori_loop(0, edge, finish, 0, unroll=2)
        more = state + 1 < 2 * STEPS
        if more:
            send(state + 1, (0, 1))
        lax.fori_loop(edge, size_x, finish, 0, unroll=2)
        if more:
            send(state + 1, (2, 3))

    for moment in range(STEPS):
        step(moment, 0, moment)
    for turn in range(STEPS):
        step(STEPS + turn, 1, STEPS - 1 - turn)
    for slot in range(2 * STEPS + 3):
        sent(slot)


def depth_matrices(size_z):
    source = lax.broadcasted_iota(jnp.int32, (size_z, size_z), 0)
    dest = lax.broadcasted_iota(jnp.int32, (size_z, size_z), 1)
    plus = jnp.zeros((size_z, size_z), jnp.float32)
    minus = plus
    for order, weight in enumerate(coeffs):
        r = order + 1
        plus = plus + jnp.where(source == dest + r, weight, 0.0)
        plus = plus - jnp.where(source == dest - r + 1, weight, 0.0)
        minus = minus + jnp.where(source == dest + r - 1, weight, 0.0)
        minus = minus - jnp.where(source == dest - r, weight, 0.0)
    return plus, minus


def window(place, amps, modulus, buoyancy, fwd_press, fwd_vel, adj_press, adj_vel, hits, recorded):
    size_x, size_y, size_z = fwd_press.shape
    tall = size_y + 2 * PAD
    plus, minus = depth_matrices(size_z)
    vmem = pl.BlockSpec(memory_space=pltpu.VMEM)
    smem = pl.BlockSpec(memory_space=pltpu.SMEM)
    field = (size_x, size_y, size_z)

    def scratch(*shape):
        return pltpu.VMEM(shape, jnp.float32)

    slots = 2 * STEPS + 3
    return pl.pallas_call(
        window_kernel,
        out_shape=jax.ShapeDtypeStruct((2,) + field, jnp.float32),
        in_specs=[smem, smem] + [vmem] * 10,
        out_specs=vmem,
        scratch_shapes=[
            scratch(2 * STEPS, size_x + 2 * RIM, tall, size_z),
            scratch(size_x + 2 * VRIM, tall, size_z),
            scratch(2, size_x + 2 * VRIM, size_y, size_z),
            scratch(2, size_x, tall, size_z),
            scratch(2, *field),
            scratch(*field),
            scratch(STEPS - 1, *field),
            scratch(STEPS, *field),
            scratch(STEPS, *field),
            scratch(STEPS, *field),
            scratch(STEPS, *field),
            pltpu.SemaphoreType.DMA((8,)),
            pltpu.SemaphoreType.DMA((slots, 4)),
            pltpu.SemaphoreType.DMA((slots, 4)),
        ],
        compiler_params=pltpu.CompilerParams(
            collective_id=0, has_side_effects=True, vmem_limit_bytes=56 * 1024 * 1024
        ),
    )(place, amps, plus, minus, modulus, buoyancy, fwd_press, fwd_vel, adj_press, adj_vel, hits, recorded)


def body(
    latent,
    w_first,
    w_second,
    fwd_press,
    fwd_vel,
    adj_press,
    adj_vel,
    src_pos,
    src_amp,
    rec_pos,
    observed,
):
    size_x, size_y = (fwd_press.shape[1], fwd_press.shape[2])
    anchor_x = lax.axis_index("gx") * size_x
    anchor_y = lax.axis_index("gy") * size_y
    depth_c, rows_x, merged = latent.shape
    size_z = fwd_press.shape[3]
    everything = gather_latent(latent.reshape(depth_c, rows_x * merged))
    all_depth = size_z // 4
    repeat = (
        lax.broadcasted_iota(jnp.int32, (all_depth, size_z), 1) // 4
        == lax.broadcasted_iota(jnp.int32, (all_depth, size_z), 0)
    ).astype(jnp.float32)
    wide = lax.dot_general(
        everything.reshape(all_depth, rows_x * merged),
        repeat,
        (((0,), (0,)), ((), ())),
        precision=exact,
    ).reshape(rows_x, merged // CH, CH, size_z)
    modulus, buoyancy, hidden, fine = decode(wide, w_first, w_second)
    hits, recorded = receiver_fields(
        rec_pos[0], observed[0], anchor_x, anchor_y, fwd_press.shape[1:]
    )
    place = jnp.stack([src_pos[0, 0] - anchor_x, src_pos[1, 0] - anchor_y, src_pos[2, 0]])
    totals = window(
        place,
        src_amp[:, 0],
        modulus,
        buoyancy,
        fwd_press[0],
        fwd_vel[0],
        adj_press[0],
        adj_vel[0],
        hits,
        recorded,
    )
    grad_wide, grad_first, grad_second = decoder_grads(
        totals, wide, hidden, fine, w_first, w_second
    )
    grad_depth = lax.dot_general(
        repeat, grad_wide.reshape(rows_x * merged, size_z), contract_lanes, precision=exact
    )
    weights = jnp.concatenate(
        [grad_second, jnp.pad(grad_first, ((0, 0), (0, 128 - CH)))], axis=0
    )
    own, weights = reduce_all(grad_depth.reshape(-1, depth_c, rows_x * merged), weights)
    return (own.reshape(latent.shape), weights[CH:, :CH], weights[:CH])


def solution(mesh):
    in_specs = (
        P("shot", "gx", "gy"),
        P(),
        P(),
        P("shot", "gx", "gy", None),
        P("shot", None, "gx", "gy", None),
        P("shot", "gx", "gy", None),
        P("shot", None, "gx", "gy", None),
        P(None, "shot"),
        P(None, "shot"),
        P("shot", None, None),
        P("shot", None, None),
    )
    out_specs = (P("shot", "gx", "gy"), P(), P())
    return jax.shard_map(body, mesh=mesh, in_specs=in_specs, out_specs=out_specs, check_vma=False)
```
